128 devices in a mesh: row: 8 (over x_hi, y), col: 16 (over x_lo, z, core).
Axes of the slice: x: 4 (x_hi: 2, x_lo: 2; x = x_hi * 2 + x_lo), y: 4, z: 4, core: 2. Of those that a mesh axis runs over, the one named last changes fastest.
Arguments:
- latent: bfloat16 [256, 81920], P('row', 'col'), may hold values from -6 to 6
- tile_reach: int32 [8, 16, 4], replicated, may hold values from 1 to 4
- first_weight: bfloat16 [3, 3, 320, 320], replicated, may hold values from -0.109375 to 0.109375
- first_bias: float32 [320], replicated, may hold values from -3 to 3
- second_weight: bfloat16 [3, 3, 320, 320], replicated, may hold values from -0.109375 to 0.109375
- second_bias: float32 [320], replicated, may hold values from -3 to 3
- proj_weight: bfloat16 [320, 512], replicated, may hold values from -0.3125 to 0.3125
- upper_weight: bfloat16 [3, 3, 512, 512], replicated, may hold values from -0.09375 to 0.09375
- upper_bias: float32 [512], replicated, may hold values from -3 to 3
- lower_weight: bfloat16 [3, 3, 512, 512], replicated, may hold values from -0.09375 to 0.09375
- lower_bias: float32 [512], replicated, may hold values from -3 to 3
Outputs:
- decoded: bfloat16 [512, 512, 512], P(('row', 'col'))
The draws below stay inside these ranges and needn't reach their ends.
All inputs are finite; a program needn't handle non-finite values.
Results may differ from the reference program's by a relative error of at most 0.0065.
Values may be sent and summed in bfloat16 or wider, within the bound.
A program may use at most 64 MiB of HBM per device.

```python
import jax
import jax.numpy as jnp
from jax import lax

C = 320
DC = 512
CH = 32
CW = 16
MARGIN = 4
NH = 256
NW = 256
N_ROW = 8
N_COL = 16


def plant(drawn, own_key, low, top_value):
    shape = drawn.shape
    spot = [jax.random.randint(jax.random.fold_in(own_key, axis), (), 0, shape[axis]) for axis in range(len(shape))]
    drawn = drawn.at[tuple(spot)].set(low)
    longest = shape.index(max(shape))
    spot[longest] = (spot[longest] + 1) % shape[longest]
    return drawn.at[tuple(spot)].set(top_value)


def block_levels(rng, dims, cuts, low, largest):
    def one(axis_at, blocks):
        steps = jax.random.uniform(jax.random.fold_in(jax.random.fold_in(rng, 6), axis_at), (blocks,), jnp.float32, low / len(cuts), largest / len(cuts))
        return jnp.repeat(jnp.exp(steps), dims[axis_at] // blocks).reshape((-1,) + (1,) * (len(dims) - axis_at - 1))

    gain = one(*cuts[0])
    for cut in cuts[1:]:
        gain = gain * one(*cut)
    return gain


def gaussian(stream_key, extent, spread, reach, split=(), kind=jnp.bfloat16):
    entries = jax.random.normal(stream_key, extent, jnp.float32) * spread
    if len(split) > 0:
        entries = block_levels(stream_key, extent, split, -0.22, 0.18) * entries
    return jnp.clip(entries, min=-reach, max=reach).astype(kind)


def setup_inputs(seed: int = 0) -> dict:
    streams_of = jax.random.split(jax.random.key(seed), 12)
    latent = gaussian(streams_of[0], (NH, NW * C), 1.0, 6.0, ((0, 8), (1, 16)))
    tile_reach = plant(jax.random.randint(streams_of[1], (N_ROW, N_COL, 4), 1, MARGIN + 1), jax.random.fold_in(streams_of[1], 1), 1, MARGIN).astype(jnp.int32)
    first_weight = gaussian(streams_of[2], (3, 3, C, C), (9 * C) ** -0.5, 0.109375)
    first_bias = gaussian(streams_of[3], (C,), 0.5, 3.0, (), jnp.float32)
    second_weight = gaussian(streams_of[4], (3, 3, C, C), (9 * C) ** -0.5, 0.109375)
    second_bias = gaussian(streams_of[5], (C,), 0.5, 3.0, (), jnp.float32)
    proj_weight = gaussian(streams_of[6], (C, DC), C ** -0.5, 0.3125)
    upper_weight = gaussian(streams_of[7], (3, 3, DC, DC), (9 * DC) ** -0.5, 0.09375)
    upper_bias = gaussian(streams_of[8], (DC,), 0.5, 3.0, (), jnp.float32)
    lower_weight = gaussian(streams_of[9], (3, 3, DC, DC), (9 * DC) ** -0.5, 0.09375)
    lower_bias = gaussian(streams_of[10], (DC,), 0.5, 3.0, (), jnp.float32)
    return dict(latent=latent, tile_reach=tile_reach, first_weight=first_weight, first_bias=first_bias, second_weight=second_weight, second_bias=second_bias, proj_weight=proj_weight, upper_weight=upper_weight, upper_bias=upper_bias, lower_weight=lower_weight, lower_bias=lower_bias)


def convolve(inputs, weight, padding):
    return lax.conv_general_dilated(inputs[None], weight, (1, 1), padding, dimension_numbers=("NHWC", "HWIO", "NHWC"), preferred_element_type=jnp.float32)[0]


def tile_block(window, window_mask, first_weight, first_bias, second_weight, second_bias):
    mask_three = window_mask[:, :, None]
    masked = window * mask_three.astype(window.dtype)
    active = (jax.nn.silu(convolve(masked, first_weight, "SAME") + first_bias) * mask_three).astype(jnp.bfloat16)
    summed = masked.astype(jnp.float32) + convolve(active, second_weight, "SAME") + second_bias
    return (summed * mask_three).astype(jnp.bfloat16)


def reference(latent, tile_reach, first_weight, first_bias, second_weight, second_bias, proj_weight, upper_weight, upper_bias, lower_weight, lower_bias):
    canvas_start = latent.reshape(NH, NW, C)
    padded = jnp.pad(canvas_start, ((MARGIN, MARGIN), (MARGIN, MARGIN), (0, 0)))
    span_rows = CH + 2 * MARGIN
    span_cols = CW + 2 * MARGIN
    offset_rows = jnp.arange(span_rows, dtype=jnp.int32) - MARGIN
    offset_cols = jnp.arange(span_cols, dtype=jnp.int32) - MARGIN

    def visit(carry, flat):
        sums, counts = carry
        row_id = flat // N_COL
        col_id = flat % N_COL
        reach_row = tile_reach[row_id, col_id]
        glob_rows = row_id * CH + offset_rows
        glob_cols = col_id * CW + offset_cols
        rows_ok = (glob_rows >= row_id * CH - reach_row[0]) & (glob_rows < (row_id + 1) * CH + reach_row[1]) & (glob_rows >= 0) & (glob_rows < NH)
        cols_ok = (glob_cols >= col_id * CW - reach_row[2]) & (glob_cols < (col_id + 1) * CW + reach_row[3]) & (glob_cols >= 0) & (glob_cols < NW)
        window_mask = (rows_ok[:, None] & cols_ok[None, :]).astype(jnp.float32)
        start_row = (row_id * CH).astype(jnp.int32)
        start_col = (col_id * CW).astype(jnp.int32)
        zero = jnp.zeros((), jnp.int32)
        window = lax.dynamic_slice(padded, (start_row, start_col, zero), (span_rows, span_cols, C))
        output = tile_block(window, window_mask, first_weight, first_bias, second_weight, second_bias)
        old_sum = lax.dynamic_slice(sums, (start_row, start_col, zero), (span_rows, span_cols, C))
        sums = lax.dynamic_update_slice(sums, old_sum + output.astype(jnp.float32), (start_row, start_col, zero))
        old_count = lax.dynamic_slice(counts, (start_row, start_col), (span_rows, span_cols))
        counts = lax.dynamic_update_slice(counts, old_count + window_mask, (start_row, start_col))
        return (sums, counts), None

    init = (jnp.zeros((NH + 2 * MARGIN, NW + 2 * MARGIN, C), jnp.float32), jnp.zeros((NH + 2 * MARGIN, NW + 2 * MARGIN), jnp.float32))
    (sums, counts), _ = lax.scan(visit, init, jnp.arange(N_ROW * N_COL, dtype=jnp.int32))
    blend = sums[MARGIN:-MARGIN, MARGIN:-MARGIN]
    canvas = (blend / counts[MARGIN:-MARGIN, MARGIN:-MARGIN, None]).astype(jnp.bfloat16)
    hidden = jnp.dot(canvas.reshape(NH * NW, C), proj_weight, preferred_element_type=jnp.float32).astype(jnp.bfloat16).reshape(NH, NW, DC)
    upsampled = jnp.repeat(jnp.repeat(hidden, 2, axis=0), 2, axis=1)
    active = jax.nn.silu(convolve(upsampled, upper_weight, "SAME") + upper_bias).astype(jnp.bfloat16)
    decoded = convolve(active, lower_weight, "SAME") + lower_bias + upsampled.astype(jnp.float32)
    return decoded.astype(jnp.bfloat16)
```

```python
import functools

import jax
import jax.numpy as jnp
from jax import lax
from jax.experimental import pallas as pl
from jax.experimental.pallas import tpu as pltpu
from jax.sharding import PartitionSpec as P

MARGIN = 4
SIDE = 8
PAD = 8
F32 = jnp.float32
BF = jnp.bfloat16
MESH = pl.DeviceIdType.MESH
VM = pl.BlockSpec(memory_space=pltpu.VMEM)
ANY = pl.BlockSpec(memory_space=pl.ANY)
SM = pl.BlockSpec(memory_space=pltpu.SMEM)
AROUND = [(dr, dc) for dr in (-1, 0, 1) for dc in (-1, 0, 1) if (dr, dc) != (0, 0)]


def peer(row, col, dr, dc):
    rows, cols = lax.axis_size("row"), lax.axis_size("col")
    return lax.rem(row + (dr + rows), rows), lax.rem(col + (dc + cols), cols)


def halo_kernel(core_ref, *refs):
    lands, (send, recv) = refs[:8], refs[8:]
    rows, cols = core_ref.shape[:2]
    row, col = lax.axis_index("row"), lax.axis_index("col")
    barrier = pltpu.get_barrier_semaphore()
    for dr, dc in AROUND:
        pl.semaphore_signal(barrier, inc=1, device_id=peer(row, col, dr, dc), device_id_type=MESH)
    pl.semaphore_wait(barrier, len(AROUND))
    copies = []
    for n, (dr, dc) in enumerate(AROUND):
        rs = {-1: pl.ds(rows - MARGIN, MARGIN), 0: pl.ds(0, rows), 1: pl.ds(0, MARGIN)}[dr]
        cs = {-1: pl.ds(cols - SIDE, SIDE), 0: pl.ds(0, cols), 1: pl.ds(0, SIDE)}[dc]
        copies.append(
            pltpu.make_async_remote_copy(
                src_ref=core_ref.at[rs, cs],
                dst_ref=lands[n],
                send_sem=send.at[n],
                recv_sem=recv.at[n],
                device_id=peer(row, col, -dr, -dc),
                device_id_type=MESH,
            )
        )
        copies[-1].start()
    for c in copies:
        c.wait()


def halo(core):
    rows, cols, ch = core.shape
    shapes = [
        jax.ShapeDtypeStruct((rows if dr == 0 else MARGIN, cols if dc == 0 else SIDE, ch), core.dtype)
        for dr, dc in AROUND
    ]
    lands = pl.pallas_call(
        halo_kernel,
        out_shape=shapes,
        in_specs=[VM],
        out_specs=[VM] * 8,
        scratch_shapes=[pltpu.SemaphoreType.DMA((8,)), pltpu.SemaphoreType.DMA((8,))],
        compiler_params=pltpu.CompilerParams(collective_id=0, has_side_effects=True),
        name="halo",
    )(core)
    got = dict(zip(AROUND, lands))
    got[0, 0] = core
    m = MARGIN
    bands = []
    for dr in (-1, 0, 1):
        bands.append(
            jnp.concatenate([got[dr, -1][:, SIDE - m :], got[dr, 0], got[dr, 1][:, :m]], axis=1)
        )
    return jnp.concatenate(bands, axis=0)


def blend_kernel(y_ref, count_ref, out_ref, *refs):
    lands, (can, send, recv, send2, recv2, self_sem) = refs[:8], refs[8:]
    rows, cols = count_ref.shape[:2]
    core = rows - 2
    row, col = lax.axis_index("row"), lax.axis_index("col")
    n_col = lax.axis_size("col")
    barrier = pltpu.get_barrier_semaphore()
    greet = [peer(row, col, 0, o) for o in range(1, n_col)]
    greet += [peer(row, col, dr, dc) for dr, dc in AROUND if dr != 0]
    for g in greet:
        pl.semaphore_signal(barrier, inc=1, device_id=g, device_id_type=MESH)
    pl.semaphore_wait(barrier, len(greet))
    m, edge = MARGIN, MARGIN + 1
    top = y_ref.shape[0]
    copies = []
    for n, (dr, dc) in enumerate(AROUND):
        rs = {-1: pl.ds(top - edge, edge), 0: pl.ds(m - 1, rows), 1: pl.ds(0, edge)}[dr]
        cs = {-1: pl.ds(SIDE + cols, SIDE), 0: pl.ds(SIDE, cols), 1: pl.ds(0, SIDE)}[dc]
        copies.append(
            pltpu.make_async_remote_copy(
                src_ref=y_ref.at[rs, cs],
                dst_ref=lands[n],
                send_sem=send.at[n],
                recv_sem=recv.at[n],
                device_id=peer(row, col, -dr, -dc),
                device_id_type=MESH,
            )
        )
        copies[-1].start()
    for c in copies:
        c.wait()
    got = dict(zip(AROUND, lands))

    def put(lo, num, middle):
        here = pl.ds(lo, num)
        total = y_ref[pl.ds(m - 1 + lo, num), SIDE : SIDE + cols].astype(F32)
        left = got[0, -1][here].astype(F32)
        right = got[0, 1][here].astype(F32)
        if not middle:
            dr = -1 if lo == 0 else 1
            total += got[dr, 0][...].astype(F32)
            left += got[dr, -1][...].astype(F32)
            right += got[dr, 1][...].astype(F32)
        total += jnp.concatenate([left, right], axis=1)
        n = count_ref[here]
        can[here] = jnp.where(n > 0, total / jnp.maximum(n, 1.0), 0.0).astype(BF)

    put(0, edge, False)
    put(edge, rows - 2 * edge, True)
    put(rows - edge, edge, False)
    mine = pl.ds(pl.multiple_of(cols * col, cols), cols)
    step = core // n_col
    deep = step + 2
    own = pltpu.make_async_copy(can.at[pl.ds(step * col, deep)], out_ref.at[:, mine], self_sem)
    own.start()
    copies = []
    for o in range(1, n_col):
        to = peer(row, col, 0, o)
        copies.append(
            pltpu.make_async_remote_copy(
                src_ref=can.at[pl.ds(step * to[1], deep)],
                dst_ref=out_ref.at[:, mine],
                send_sem=send2.at[o],
                recv_sem=recv2.at[o],
                device_id=to,
                device_id_type=MESH,
            )
        )
        copies[-1].start()
    own.wait()
    for o in range(1, n_col):
        copies[o - 1].wait_send()
        src = peer(row, col, 0, -o)
        pltpu.make_async_remote_copy(
            src_ref=can.at[pl.ds(0, deep)],
            dst_ref=out_ref.at[:, pl.ds(pl.multiple_of(cols * src[1], cols), cols)],
            send_sem=send2.at[o],
            recv_sem=recv2.at[o],
            device_id=src,
            device_id_type=MESH,
        ).wait_recv()


def blend(y, count):
    rows, cols = count.shape[:2]
    ch = y.shape[2]
    n_col = lax.axis_size("col")
    shapes = [
        pltpu.VMEM((rows if dr == 0 else MARGIN + 1, cols if dc == 0 else SIDE, ch), BF) for dr, dc in AROUND
    ]
    deep = (rows - 2) // n_col + 2
    return pl.pallas_call(
        blend_kernel,
        out_shape=jax.ShapeDtypeStruct((deep, n_col * cols, ch), BF),
        in_specs=[VM, VM],
        out_specs=VM,
        scratch_shapes=shapes
        + [
            pltpu.VMEM((rows, cols, ch), BF),
            pltpu.SemaphoreType.DMA((8,)),
            pltpu.SemaphoreType.DMA((8,)),
            pltpu.SemaphoreType.DMA((n_col,)),
            pltpu.SemaphoreType.DMA((n_col,)),
            pltpu.SemaphoreType.DMA,
        ],
        compiler_params=pltpu.CompilerParams(collective_id=1, has_side_effects=True),
        name="blend",
    )(y, count)


def spread(g):
    outer = 0.5 * (g[0] + g[2])
    mid = 0.5 * g[1]
    return [g[0], outer + mid, outer - mid, g[2]]


def weights_kernel(up_ref, lo_ref, uo_ref, lo_out_ref):
    rows, d = up_ref.shape[2:]

    def chunk(n, _):
        sl = pl.ds(pl.multiple_of(n * 16, 16), 16)
        for lane in range(0, d, 128):
            ln = slice(lane, lane + 128)
            cols = []
            for b in range(3):
                w = [up_ref[a, b, sl, ln].astype(F32) for a in range(3)]
                cols.append([w[0], w[0] + w[1] + w[2], w[2]])
            for p in range(3):
                v = [cols[0][p], cols[0][p] + cols[1][p] + cols[2][p], cols[2][p]]
                for q in range(3):
                    uo_ref[3 * p + q, sl, ln] = v[q].astype(BF)
            cols = [spread([lo_ref[a, b, sl, ln].astype(F32) for a in range(3)]) for b in range(3)]
            for r in range(4):
                v = spread([cols[b][r] for b in range(3)])
                for c in range(4):
                    lo_out_ref[4 * r + c, sl, ln] = v[c].astype(BF)
        return 0

    lax.fori_loop(0, rows // 16, chunk, 0)


def transform_weights(upper, lower):
    d = upper.shape[2]
    step = 64
    return pl.pallas_call(
        weights_kernel,
        grid=(d // step,),
        in_specs=[pl.BlockSpec((3, 3, step, d), lambda i: (0, 0, i, 0))] * 2,
        out_specs=[pl.BlockSpec((9, step, d), lambda i: (0, i, 0)), pl.BlockSpec((16, step, d), lambda i: (0, i, 0))],
        out_shape=[jax.ShapeDtypeStruct((9, d, d), BF), jax.ShapeDtypeStruct((16, d, d), BF)],
        compiler_params=pltpu.CompilerParams(vmem_limit_bytes=48 * 2**20),
        cost_estimate=pl.CostEstimate(flops=20 * 9 * d * d, bytes_accessed=2 * (18 + 25) * d * d, transcendentals=0),
        name="weights",
    )(upper, lower)


def dot(a, b):
    return jnp.dot(a, b, preferred_element_type=F32)


def decode_kernel(cols, d, keep_ref, can_ref, proj_ref, uup_hbm, bup_ref, ulo_hbm, blo_ref, out_ref,
                  hid, act, ts, acc, inter, uup, ulo, upsem, losem):
    upc = [pltpu.make_async_copy(uup_hbm.at[i], uup.at[i], upsem.at[i]) for i in range(9)]
    loc = [pltpu.make_async_copy(ulo_hbm.at[i], ulo.at[i], losem.at[i]) for i in range(16)]
    for i in (3, 4, 5, 6, 7, 8, 0, 1, 2):
        upc[i].start()
    for c in loc:
        c.start()
    body = pl.ds(PAD, cols)
    prev = pl.ds(PAD - 1, cols)
    nxt = pl.ds(PAD + 1, cols)
    zero8 = jnp.zeros((4, PAD, d), F32)
    hid[:, 0:PAD, :] = zero8
    hid[:, PAD + cols:, :] = zero8
    zact = jnp.zeros((6, 2, PAD, d), F32)
    act[:, :, 0:PAD, :] = zact
    act[:, :, PAD + cols:, :] = zact
    for i in range(4):
        v = dot(can_ref[i], proj_ref[...]).astype(BF).astype(F32)
        hid[i, body, :] = v

    def three(load):
        mid = load(body)
        return [(load(prev) - mid).astype(BF), mid.astype(BF), (load(nxt) - mid).astype(BF)]

    def both(x, p):
        s = dot(x[1], uup[3 * p + 1])
        return s + dot(x[0], uup[3 * p]), s + dot(x[2], uup[3 * p + 2])

    for i in (3, 4, 5):
        upc[i].wait()
    e, o = both(three(lambda sl: hid[0, sl, :]), 1)
    ts[0, 0] = e
    ts[0, 1] = o
    for i in (6, 7, 8, 0, 1, 2):
        upc[i].wait()

    def act_row(slot, src, pair, keep):
        for par in range(2):
            v = src[par] + pair[par] + bup_ref[...]
            a = v / (1.0 + jnp.exp(-v))
            a = a.astype(BF).astype(F32)
            act[slot, par, body, :] = jnp.where(keep, a, 0.0)

    def step(k, _):
        x = three(lambda sl: hid[k + 1, sl, :] - hid[k, sl, :])
        down = both(x, 2)
        act_row(2 * k, (ts[k % 2, 0], ts[k % 2, 1]), down, (keep_ref[0] > 0) | (k > 0))
        cur = both(three(lambda sl: hid[k + 1, sl, :]), 1)
        ts[(k + 1) % 2, 0] = cur[0]
        ts[(k + 1) % 2, 1] = cur[1]
        up = both(x, 0)
        act_row(2 * k + 1, cur, (-up[0], -up[1]), (keep_ref[1] > 0) | (k < 2))
        return 0

    lax.fori_loop(0, 3, step, 0)
    for c in loc:
        c.wait()

    for t in range(2):
        h = hid[t + 1, body, :] + blo_ref[...]
        for a in range(2):
            for b in range(2):
                acc[t, a, b] = h

    def row_step(r, _):
        first = jnp.where(r == 0, 0, jnp.where(r == 2, 2, 1))
        second = jnp.where(r == 3, 3, jnp.where(r == 2, 1, 2))
        sgn = jnp.where(r == 1, 1.0, -1.0).astype(F32)
        s0 = jnp.where(r == 3, 0.0, 1.0).astype(F32)
        s1 = jnp.where(r == 0, 0.0, jnp.where(r == 1, 1.0, -1.0)).astype(F32)
        vs = [[], [], [], []]
        for t in range(2):
            def ld(par, sl):
                return act[2 * t + first, par, sl, :] + sgn * act[2 * t + second, par, sl, :]
            ev = ld(0, body)
            od = ld(1, body)
            vs[0].append((ld(1, prev) - od).astype(BF))
            vs[1].append((ev + od).astype(BF))
            vs[2].append((od - ev).astype(BF))
            vs[3].append((ev - ld(0, nxt)).astype(BF))
        m = [dot(jnp.concatenate(vs[c], axis=0), ulo[4 * r + c]) for c in range(4)]
        plus, minus = m[1] + m[2], m[1] - m[2]
        y = [plus + m[0], minus - m[3]]
        for t in range(2):
            for b in range(2):
                part = y[b][t * cols:(t + 1) * cols]
                acc[t, 0, b] += s0 * part
                acc[t, 1, b] += s1 * part
        return 0

    lax.fori_loop(0, 4, row_step, 0)
    for t in range(2):
        for a in range(2):
            for b in range(2):
                for lane in range(0, d, 128):
                    inter[lane // 128, pl.ds(b, cols, stride=2), :] = acc[t, a, b, :, lane:lane + 128]
            for lane in range(0, d, 128):
                out_ref[2 * t + a, :, lane:lane + 128] = inter[lane // 128].astype(BF)


def decode(keep, canvas, proj, uup, bup, ulo, blo):
    cols, d = canvas.shape[1], proj.shape[1]
    return pl.pallas_call(
        functools.partial(decode_kernel, cols, d),
        out_shape=jax.ShapeDtypeStruct((4, 2 * cols, d), BF),
        in_specs=[SM, VM, VM, ANY, VM, ANY, VM],
        out_specs=VM,
        scratch_shapes=[
            pltpu.VMEM((4, cols + 2 * PAD, d), F32),
            pltpu.VMEM((6, 2, cols + 2 * PAD, d), F32),
            pltpu.VMEM((2, 2, cols, d), F32),
            pltpu.VMEM((2, 2, 2, cols, d), F32),
            pltpu.VMEM((d // 128, 2 * cols, 128), F32),
            pltpu.VMEM((9, d, d), BF),
            pltpu.VMEM((16, d, d), BF),
            pltpu.SemaphoreType.DMA((9,)),
            pltpu.SemaphoreType.DMA((16,)),
        ],
        compiler_params=pltpu.CompilerParams(vmem_limit_bytes=60 * 2**20),
        name="decode",
    )(keep, canvas, proj, uup, bup, ulo, blo)


def convolve(inputs, weight):
    return lax.conv_general_dilated(
        inputs[None],
        weight,
        (1, 1),
        "SAME",
        dimension_numbers=("NHWC", "HWIO", "NHWC"),
        preferred_element_type=F32,
    )[0]


def on_device(
    latent,
    tile_reach,
    first_weight,
    first_bias,
    second_weight,
    second_bias,
    proj_weight,
    upper_weight,
    upper_bias,
    lower_weight,
    lower_bias,
):
    chans = first_weight.shape[2]
    rows = latent.shape[0]
    cols = latent.shape[1] // chans
    m = MARGIN
    n_row = lax.axis_size("row")
    n_col = lax.axis_size("col")
    row_id = lax.axis_index("row")
    col_id = lax.axis_index("col")
    total_rows = rows * n_row
    total_cols = cols * n_col
    uup, ulo = transform_weights(upper_weight, lower_weight)
    window = halo(latent.reshape(rows, cols, chans))
    reach = tile_reach[row_id, col_id]
    glob_rows = row_id * rows - m + jnp.arange(rows + 2 * m, dtype=jnp.int32)
    glob_cols = col_id * cols - m + jnp.arange(cols + 2 * m, dtype=jnp.int32)
    rows_ok = (
        (glob_rows >= row_id * rows - reach[0])
        & (glob_rows < (row_id + 1) * rows + reach[1])
        & (glob_rows >= 0)
        & (glob_rows < total_rows)
    )
    cols_ok = (
        (glob_cols >= col_id * cols - reach[2])
        & (glob_cols < (col_id + 1) * cols + reach[3])
        & (glob_cols >= 0)
        & (glob_cols < total_cols)
    )
    mask = (rows_ok[:, None] & cols_ok[None, :])[:, :, None]
    masked = jnp.where(mask, window, 0)
    active = jnp.where(mask, jax.nn.silu(convolve(masked, first_weight) + first_bias), 0.0).astype(BF)
    output = jnp.where(
        mask, masked.astype(F32) + convolve(active, second_weight) + second_bias, 0.0
    ).astype(BF)
    wide = jnp.pad(output, ((0, 0), (SIDE - m, SIDE - m), (0, 0)))
    grid_rows = jnp.arange(n_row, dtype=jnp.int32)[:, None]
    grid_cols = jnp.arange(n_col, dtype=jnp.int32)[None, :]
    low_rows = (grid_rows * rows - tile_reach[:, :, 0])[:, :, None, None]
    high_rows = ((grid_rows + 1) * rows + tile_reach[:, :, 1])[:, :, None, None]
    low_cols = (grid_cols * cols - tile_reach[:, :, 2])[:, :, None, None]
    high_cols = ((grid_cols + 1) * cols + tile_reach[:, :, 3])[:, :, None, None]
    core_rows = (row_id * rows - 1 + jnp.arange(rows + 2, dtype=jnp.int32))[None, None, :, None]
    core_cols = (col_id * cols + jnp.arange(cols, dtype=jnp.int32))[None, None, None, :]
    inside = (
        (core_rows >= jnp.maximum(low_rows, 0))
        & (core_rows < jnp.minimum(high_rows, total_rows))
        & (core_cols >= low_cols)
        & (core_cols < high_cols)
    )
    count = jnp.sum(inside.astype(F32), axis=(0, 1))[:, :, None]
    canvas = blend(wide, count)
    keep = jnp.stack(
        [
            ((row_id > 0) | (col_id > 0)).astype(jnp.int32),
            ((row_id < n_row - 1) | (col_id < n_col - 1)).astype(jnp.int32),
        ]
    )
    return decode(keep, canvas, proj_weight, uup, upper_bias[None], ulo, lower_bias[None])


def solution(mesh):
    in_specs = (P("row", "col"), P(), P(), P(), P(), P(), P(), P(), P(), P(), P())
    out_specs = P(("row", "col"), None, None)
    return jax.shard_map(on_device, mesh=mesh, in_specs=in_specs, out_specs=out_specs, check_vma=False)
```

```python
import functools

import jax
import jax.numpy as jnp
from jax import lax
from jax.experimental import pallas as pl
from jax.experimental.pallas import tpu as pltpu
from jax.sharding import PartitionSpec as P

MARGIN = 4
SIDE = 8
PAD = 8
F32 = jnp.float32
BF = jnp.bfloat16
MESH = pl.DeviceIdType.MESH
VM = pl.BlockSpec(memory_space=pltpu.VMEM)
HB = pl.BlockSpec(memory_space=pltpu.HBM)
SM = pl.BlockSpec(memory_space=pltpu.SMEM)
AROUND = [(dr, dc) for dr in (-1, 0, 1) for dc in (-1, 0, 1) if (dr, dc) != (0, 0)]


def dot(a, b):
    return jnp.dot(a, b, preferred_element_type=F32)


def peer(row, col, dr, dc):
    rows, cols = lax.axis_size("row"), lax.axis_size("col")
    return lax.rem(row + (dr + rows), rows), lax.rem(col + (dc + cols), cols)


def halo_kernel(core_ref, *refs):
    lands, (send, recv) = refs[:8], refs[8:]
    rows, cols = core_ref.shape[:2]
    row, col = lax.axis_index("row"), lax.axis_index("col")
    barrier = pltpu.get_barrier_semaphore()
    for dr, dc in AROUND:
        pl.semaphore_signal(barrier, inc=1, device_id=peer(row, col, dr, dc), device_id_type=MESH)
    pl.semaphore_wait(barrier, len(AROUND))
    copies = []
    for n, (dr, dc) in enumerate(AROUND):
        rs = {-1: pl.ds(rows - MARGIN, MARGIN), 0: pl.ds(0, rows), 1: pl.ds(0, MARGIN)}[dr]
        cs = {-1: pl.ds(cols - SIDE, SIDE), 0: pl.ds(0, cols), 1: pl.ds(0, SIDE)}[dc]
        copies.append(
            pltpu.make_async_remote_copy(
                src_ref=core_ref.at[rs, cs],
                dst_ref=lands[n],
                send_sem=send.at[n],
                recv_sem=recv.at[n],
                device_id=peer(row, col, -dr, -dc),
                device_id_type=MESH,
            )
        )
        copies[-1].start()
    for c in copies:
        c.wait()


def halo(core):
    rows, cols, ch = core.shape
    shapes = [
        jax.ShapeDtypeStruct((rows if dr == 0 else MARGIN, cols if dc == 0 else SIDE, ch), core.dtype)
        for dr, dc in AROUND
    ]
    lands = pl.pallas_call(
        halo_kernel,
        out_shape=shapes,
        in_specs=[VM],
        out_specs=[VM] * 8,
        scratch_shapes=[pltpu.SemaphoreType.DMA((8,)), pltpu.SemaphoreType.DMA((8,))],
        compiler_params=pltpu.CompilerParams(collective_id=0, has_side_effects=True),
        name="halo",
    )(core)
    return lands


def place(reach_ref, row, col, dr, dc, rows, cols):
    n_row, n_col = lax.axis_size("row"), lax.axis_size("col")
    there = (row + dr >= 0) & (row + dr < n_row) & (col + dc >= 0) & (col + dc < n_col)
    r = lax.rem(row + (dr + n_row), n_row)
    c = lax.rem(col + (dc + n_col), n_col)
    low_r = jnp.maximum((row + dr) * rows - reach_ref[r, c, 0], 0)
    high_r = jnp.minimum((row + dr + 1) * rows + reach_ref[r, c, 1], rows * n_row)
    low_c = jnp.maximum((col + dc) * cols - reach_ref[r, c, 2], 0)
    high_c = jnp.minimum((col + dc + 1) * cols + reach_ref[r, c, 3], cols * n_col)
    return low_r, jnp.where(there, high_r, low_r), low_c, high_c


def tile_kernel(reach_ref, core_ref, *refs):
    lands = refs[:8]
    w1_hbm, b1_ref, w2_hbm, b2_ref, y_ref, x, act, ga, gb, rest, w1, w2, r1, r2, wsem = refs[8:]
    rows, cols, ch = core_ref.shape
    m = MARGIN
    high, wide, span = rows + 2 * m, cols + 2 * SIDE, cols + 2 * m
    main = ch // 128 * 128
    left = ch - main
    wc = [pltpu.make_async_copy(src, dst, wsem.at[n]) for n, (src, dst) in enumerate(((w1_hbm, w1), (w2_hbm, w2)))]
    for c in wc:
        c.start()
    row, col = lax.axis_index("row"), lax.axis_index("col")
    low_r, high_r, low_c, high_c = place(reach_ref, row, col, 0, 0, rows, cols)
    got = dict(zip(AROUND, lands))
    got[0, 0] = core_ref
    top, start = row * rows - m, col * cols - SIDE
    cid = lax.broadcasted_iota(jnp.int32, (1, wide, ch), 1) + start
    cols_ok = (cid >= low_c) & (cid < high_c)

    def masked(value, at):
        rid = lax.broadcasted_iota(jnp.int32, value.shape, 0) + (top + at)
        ok = (rid >= low_r) & (rid < high_r) & cols_ok
        return jnp.where(ok, value, 0.0)

    def fill(dr, at, num, src):
        sides = [got[dr, dc][pl.ds(src, num)].astype(F32) for dc in (-1, 0, 1)]
        x[pl.ds(at + 1, num)] = masked(jnp.concatenate(sides, axis=1), at)

    fill(-1, 0, m, 0)
    part = 8

    def fill_core(n, _):
        fill(0, m + part * n, part, part * n)
        return 0

    lax.fori_loop(0, rows // part, fill_core, 0)
    fill(1, m + rows, m, 0)
    for buf in (x, act):
        buf[0] = jnp.zeros((wide, ch), F32)
        buf[high + 1] = jnp.zeros((wide, ch), F32)

    def clear(n, _):
        act[pl.ds(part * n + 1, part), 0:8, :] = jnp.zeros((part, 8, ch), F32)
        act[pl.ds(part * n + 1, part), wide - 8 : wide, :] = jnp.zeros((part, 8, ch), F32)
        return 0

    lax.fori_loop(0, high // part, clear, 0)
    base = SIDE - m

    def gather(buf):
        def pair(n, _):
            pieces = [
                buf[pl.ds(2 * n, 2), base + dc : base + dc + span, :].reshape(2 * span, ch) for dc in (-1, 0, 1)
            ]
            v = jnp.concatenate(pieces, axis=1).astype(BF)
            ga[pl.ds(pl.multiple_of(2 * span * n, 16), 2 * span), :] = v
            return 0

        def odd(n, _):
            pieces = [
                buf[pl.ds(2 * n + 1, 2), base + dc : base + dc + span, :].reshape(2 * span, ch) for dc in (-1, 0, 1)
            ]
            v = jnp.concatenate(pieces, axis=1).astype(BF)
            gb[pl.ds(pl.multiple_of(2 * span * n, 16), 2 * span), :] = v
            return 0

        lax.fori_loop(0, (high + 2) // 2, pair, 0)
        lax.fori_loop(0, high // 2, odd, 0)

    def narrow(w, r):
        r[...] = jnp.concatenate([w[dr, :, main:] for dr in range(3)], axis=1)

    half = high // 2
    count = half * span

    def conv(w, r, b_ref, finish):
        for n in range(2):
            size = (high + 2) // 2 * span
            rest[pl.ds(n * size, size), :] = dot(ga[pl.ds(n * size, size), :], r[...])

        def chunk(n, _):
            at = pl.multiple_of(n * count, 16)
            big = (
                dot(ga[pl.ds(at, count), :], w[0, :, :main])
                + dot(gb[pl.ds(at, count), :], w[1, :, :main])
                + dot(ga[pl.ds(pl.multiple_of(at + 2 * span, 16), count), :], w[2, :, :main])
            )
            finish(n, 0, main, big + b_ref[:, :main])
            small = (
                rest[pl.ds(at, count), :left]
                + rest[pl.ds(pl.multiple_of(at + span, 8), count), left : 2 * left]
                + rest[pl.ds(pl.multiple_of(at + 2 * span, 8), count), 2 * left :]
            )
            finish(n, main, ch, small + b_ref[:, main:])
            return 0

        lax.fori_loop(0, 2, chunk, 0)

    def window_mask(n, width):
        shape = (half, span, width)
        rid = lax.broadcasted_iota(jnp.int32, shape, 0) + (top + n * half)
        kid = lax.broadcasted_iota(jnp.int32, shape, 1) + (start + base)
        return (rid >= low_r) & (rid < high_r) & (kid >= low_c) & (kid < high_c)

    def first(n, lo, hi, v):
        v = (v / (1.0 + jnp.exp(-v))).reshape(half, span, hi - lo)
        v = jnp.where(window_mask(n, hi - lo), v, 0.0)
        act[pl.ds(n * half + 1, half), base : base + span, lo:hi] = v

    def second(n, lo, hi, v):
        here = pl.ds(n * half + 1, half)
        v = v.reshape(half, span, hi - lo) + x[here, base : base + span, lo:hi]
        act[here, base : base + span, lo:hi] = jnp.where(window_mask(n, hi - lo), v, 0.0)

    gather(x)
    wc[0].wait()
    narrow(w1, r1)
    conv(w1, r1, b1_ref, first)
    gather(act)
    wc[1].wait()
    narrow(w2, r2)
    conv(w2, r2, b2_ref, second)

    def emit(n, _):
        y_ref[pl.ds(part * n, part)] = act[pl.ds(part * n + 1, part)].astype(BF)
        return 0

    lax.fori_loop(0, high // part, emit, 0)


def tiles(reach, core, lands, w1, b1, w2, b2):
    rows, cols, ch = core.shape
    high, wide, span = rows + 2 * MARGIN, cols + 2 * SIDE, cols + 2 * MARGIN
    left = 3 * (ch % 128)
    w1, w2 = (w.reshape(3, 3 * ch, ch) for w in (w1, w2))
    return pl.pallas_call(
        tile_kernel,
        out_shape=jax.ShapeDtypeStruct((high, wide, ch), BF),
        in_specs=[SM] + [VM] * 9 + [HB, VM, HB, VM],
        out_specs=VM,
        scratch_shapes=[
            pltpu.VMEM((high + 2, wide, ch), F32),
            pltpu.VMEM((high + 2, wide, ch), F32),
            pltpu.VMEM(((high + 2) * span, 3 * ch), BF),
            pltpu.VMEM((high * span, 3 * ch), BF),
            pltpu.VMEM(((high + 2) * span, left), F32),
            pltpu.VMEM((3, 3 * ch, ch), BF),
            pltpu.VMEM((3, 3 * ch, ch), BF),
            pltpu.VMEM((3 * ch, left), BF),
            pltpu.VMEM((3 * ch, left), BF),
            pltpu.SemaphoreType.DMA((2,)),
        ],
        compiler_params=pltpu.CompilerParams(vmem_limit_bytes=48 * 2**20),
        name="tiles",
    )(reach, core, *lands, w1, b1, w2, b2)


def spread(g):
    outer = 0.5 * (g[0] + g[2])
    mid = 0.5 * g[1]
    return [g[0], outer + mid, outer - mid, g[2]]


def upper_forms(up, out, sl, ln):
    cols = []
    for b in range(3):
        w = [up[a, b, sl, ln].astype(F32) for a in range(3)]
        cols.append([w[0], w[0] + w[1] + w[2], w[2]])
    for p in range(3):
        v = [cols[0][p], cols[0][p] + cols[1][p] + cols[2][p], cols[2][p]]
        for q in range(3):
            out[3 * p + q, sl, ln] = v[q].astype(BF)


def lower_forms(lo, out, sl, ln):
    cols = [spread([lo[a, b, sl, ln].astype(F32) for a in range(3)]) for b in range(3)]
    for r in range(4):
        v = spread([cols[b][r] for b in range(3)])
        for c in range(4):
            out[4 * r + c, sl, ln] = v[c].astype(BF)


def blend_kernel(reach_ref, y_ref, up_hbm, lo_hbm, out_ref, uo_hbm, vo_hbm, *refs):
    lands = refs[:8]
    can, count, up, lo, uo, vo, send, recv, send2, recv2, self_sem, wsem, usem, vsem = refs[8:]
    rows, cols, ch = can.shape
    core = rows - 2
    loads = [pltpu.make_async_copy(up_hbm, up, wsem.at[0]), pltpu.make_async_copy(lo_hbm, lo, wsem.at[1])]
    for c in loads:
        c.start()
    row, col = lax.axis_index("row"), lax.axis_index("col")
    n_col = lax.axis_size("col")
    barrier = pltpu.get_barrier_semaphore()
    greet = [peer(row, col, 0, o) for o in range(1, n_col)]
    greet += [peer(row, col, dr, dc) for dr, dc in AROUND if dr != 0]
    for g in greet:
        pl.semaphore_signal(barrier, inc=1, device_id=g, device_id_type=MESH)
    pl.semaphore_wait(barrier, len(greet))
    m, edge = MARGIN, MARGIN + 1
    top = y_ref.shape[0]
    copies = []
    for n, (dr, dc) in enumerate(AROUND):
        rs = {-1: pl.ds(top - edge, edge), 0: pl.ds(m - 1, rows), 1: pl.ds(0, edge)}[dr]
        cs = {-1: pl.ds(SIDE + cols, SIDE), 0: pl.ds(SIDE, cols), 1: pl.ds(0, SIDE)}[dc]
        copies.append(
            pltpu.make_async_remote_copy(
                src_ref=y_ref.at[rs, cs],
                dst_ref=lands[n],
                send_sem=send.at[n],
                recv_sem=recv.at[n],
                device_id=peer(row, col, -dr, -dc),
                device_id_type=MESH,
            )
        )
        copies[-1].start()
    shape = count.shape
    rid = lax.broadcasted_iota(jnp.int32, shape, 0) + (row * core - 1)
    cid = lax.broadcasted_iota(jnp.int32, shape, 1) + col * cols
    total = jnp.zeros(shape, F32)
    for dr in (-1, 0, 1):
        for dc in (-1, 0, 1):
            low_r, high_r, low_c, high_c = place(reach_ref, row, col, dr, dc, core, cols)
            inside = (rid >= low_r) & (rid < high_r) & (cid >= low_c) & (cid < high_c)
            total += jnp.where(inside, 1.0, 0.0)
    count[...] = total
    for c in copies:
        c.wait()
    got = dict(zip(AROUND, lands))

    def put(lo, num, middle):
        here = pl.ds(lo, num)
        total = y_ref[pl.ds(m - 1 + lo, num), SIDE : SIDE + cols].astype(F32)
        left = got[0, -1][here].astype(F32)
        right = got[0, 1][here].astype(F32)
        if not middle:
            dr = -1 if lo == 0 else 1
            total += got[dr, 0][...].astype(F32)
            left += got[dr, -1][...].astype(F32)
            right += got[dr, 1][...].astype(F32)
        total += jnp.concatenate([left, right], axis=1)
        n = count[here][:, :, :1]
        can[here] = jnp.where(n > 0, total / jnp.maximum(n, 1.0), 0.0).astype(BF)

    put(0, edge, False)
    put(edge, rows - 2 * edge, True)
    put(rows - edge, edge, False)
    mine = pl.ds(pl.multiple_of(cols * col, cols), cols)
    step = core // n_col
    deep = step + 2
    own = pltpu.make_async_copy(can.at[pl.ds(step * col, deep)], out_ref.at[:, mine], self_sem)
    own.start()
    copies = []
    for o in range(1, n_col):
        to = peer(row, col, 0, o)
        copies.append(
            pltpu.make_async_remote_copy(
                src_ref=can.at[pl.ds(step * to[1], deep)],
                dst_ref=out_ref.at[:, mine],
                send_sem=send2.at[o],
                recv_sem=recv2.at[o],
                device_id=to,
                device_id_type=MESH,
            )
        )
        copies[-1].start()
    for c in loads:
        c.wait()
    depth, width = up.shape[2:]
    block = 64
    stores = []

    def forms(form, src, dst, dst_hbm, sem):
        def load(n):
            sl = pl.ds(pl.multiple_of(n * block, block), block)
            return pltpu.make_async_copy(dst.at[:, sl], dst_hbm.at[:, sl], sem.at[n])

        def body(n, _):
            def inner(k, _):
                sl = pl.ds(pl.multiple_of(n * block + k * 16, 16), 16)
                for lane in range(0, width, 128):
                    form(src, dst, sl, slice(lane, lane + 128))
                return 0

            lax.fori_loop(0, block // 16, inner, 0)
            load(n).start()
            return 0

        lax.fori_loop(0, depth // block, body, 0)
        stores.extend(load(n) for n in range(depth // block))

    forms(upper_forms, up, uo, uo_hbm, usem)
    forms(lower_forms, lo, vo, vo_hbm, vsem)
    for c in stores:
        c.wait()
    own.wait()
    for o in range(1, n_col):
        copies[o - 1].wait_send()
        src = peer(row, col, 0, -o)
        pltpu.make_async_remote_copy(
            src_ref=can.at[pl.ds(0, deep)],
            dst_ref=out_ref.at[:, pl.ds(pl.multiple_of(cols * src[1], cols), cols)],
            send_sem=send2.at[o],
            recv_sem=recv2.at[o],
            device_id=src,
            device_id_type=MESH,
        ).wait_recv()


def blend(reach, y, rows, cols, upper, lower):
    ch = y.shape[2]
    d = upper.shape[2]
    n_col = lax.axis_size("col")
    tall = rows + 2
    deep = rows // n_col + 2
    shapes = [
        pltpu.VMEM((tall if dr == 0 else MARGIN + 1, cols if dc == 0 else SIDE, ch), BF) for dr, dc in AROUND
    ]
    return pl.pallas_call(
        blend_kernel,
        out_shape=[
            jax.ShapeDtypeStruct((deep, n_col * cols, ch), BF),
            jax.ShapeDtypeStruct((9, d, d), BF),
            jax.ShapeDtypeStruct((16, d, d), BF),
        ],
        in_specs=[SM, VM, HB, HB],
        out_specs=[VM, HB, HB],
        scratch_shapes=shapes
        + [
            pltpu.VMEM((tall, cols, ch), BF),
            pltpu.VMEM((tall, cols, 128), F32),
            pltpu.VMEM((3, 3, d, d), BF),
            pltpu.VMEM((3, 3, d, d), BF),
            pltpu.VMEM((9, d, d), BF),
            pltpu.VMEM((16, d, d), BF),
            pltpu.SemaphoreType.DMA((8,)),
            pltpu.SemaphoreType.DMA((8,)),
            pltpu.SemaphoreType.DMA((n_col,)),
            pltpu.SemaphoreType.DMA((n_col,)),
            pltpu.SemaphoreType.DMA,
            pltpu.SemaphoreType.DMA((2,)),
            pltpu.SemaphoreType.DMA((d // 64,)),
            pltpu.SemaphoreType.DMA((d // 64,)),
        ],
        compiler_params=pltpu.CompilerParams(
            collective_id=1, has_side_effects=True, vmem_limit_bytes=48 * 2**20
        ),
        name="blend",
    )(reach, y, upper, lower)


def decode_kernel(cols, d, can_ref, proj_ref, uup_hbm, bup_ref, ulo_hbm, blo_ref, out_ref,
                  hid, act, ts, acc, inter, uup, ulo, upsem, losem):
    row, col = lax.axis_index("row"), lax.axis_index("col")
    first_dev = (row == 0) & (col == 0)
    last_dev = (row == lax.axis_size("row") - 1) & (col == lax.axis_size("col") - 1)
    upc = [pltpu.make_async_copy(uup_hbm.at[i], uup.at[i], upsem.at[i]) for i in range(9)]
    loc = [pltpu.make_async_copy(ulo_hbm.at[i], ulo.at[i], losem.at[i]) for i in range(16)]
    for i in (3, 4, 5, 6, 7, 8, 0, 1, 2):
        upc[i].start()
    for c in loc:
        c.start()
    body = pl.ds(PAD, cols)
    prev = pl.ds(PAD - 1, cols)
    nxt = pl.ds(PAD + 1, cols)
    zero8 = jnp.zeros((4, PAD, d), F32)
    hid[:, 0:PAD, :] = zero8
    hid[:, PAD + cols:, :] = zero8
    zact = jnp.zeros((6, 2, PAD, d), F32)
    act[:, :, 0:PAD, :] = zact
    act[:, :, PAD + cols:, :] = zact
    for i in range(4):
        v = dot(can_ref[i], proj_ref[...]).astype(BF).astype(F32)
        hid[i, body, :] = v

    def three(load):
        mid = load(body)
        return [(load(prev) - mid).astype(BF), mid.astype(BF), (load(nxt) - mid).astype(BF)]

    def both(x, p):
        s = dot(x[1], uup[3 * p + 1])
        return s + dot(x[0], uup[3 * p]), s + dot(x[2], uup[3 * p + 2])

    for i in (3, 4, 5):
        upc[i].wait()
    e, o = both(three(lambda sl: hid[0, sl, :]), 1)
    ts[0, 0] = e
    ts[0, 1] = o
    for i in (6, 7, 8, 0, 1, 2):
        upc[i].wait()

    def act_row(slot, src, pair, keep):
        for par in range(2):
            v = src[par] + pair[par] + bup_ref[...]
            a = v / (1.0 + jnp.exp(-v))
            a = a.astype(BF).astype(F32)
            act[slot, par, body, :] = jnp.where(keep, a, 0.0)

    def step(k, _):
        x = three(lambda sl: hid[k + 1, sl, :] - hid[k, sl, :])
        down = both(x, 2)
        act_row(2 * k, (ts[k % 2, 0], ts[k % 2, 1]), down, jnp.logical_not(first_dev) | (k > 0))
        cur = both(three(lambda sl: hid[k + 1, sl, :]), 1)
        ts[(k + 1) % 2, 0] = cur[0]
        ts[(k + 1) % 2, 1] = cur[1]
        up = both(x, 0)
        act_row(2 * k + 1, cur, (-up[0], -up[1]), jnp.logical_not(last_dev) | (k < 2))
        return 0

    lax.fori_loop(0, 3, step, 0)
    for c in loc:
        c.wait()

    for t in range(2):
        h = hid[t + 1, body, :] + blo_ref[...]
        for a in range(2):
            for b in range(2):
                acc[t, a, b] = h

    def row_step(r, _):
        first = jnp.where(r == 0, 0, jnp.where(r == 2, 2, 1))
        second = jnp.where(r == 3, 3, jnp.where(r == 2, 1, 2))
        sgn = jnp.where(r == 1, 1.0, -1.0).astype(F32)
        s0 = jnp.where(r == 3, 0.0, 1.0).astype(F32)
        s1 = jnp.where(r == 0, 0.0, jnp.where(r == 1, 1.0, -1.0)).astype(F32)
        vs = [[], [], [], []]
        for t in range(2):
            def ld(par, sl):
                return act[2 * t + first, par, sl, :] + sgn * act[2 * t + second, par, sl, :]
            ev = ld(0, body)
            od = ld(1, body)
            vs[0].append((ld(1, prev) - od).astype(BF))
            vs[1].append((ev + od).astype(BF))
            vs[2].append((od - ev).astype(BF))
            vs[3].append((ev - ld(0, nxt)).astype(BF))
        m = [dot(jnp.concatenate(vs[c], axis=0), ulo[4 * r + c]) for c in range(4)]
        plus, minus = m[1] + m[2], m[1] - m[2]
        y = [plus + m[0], minus - m[3]]
        for t in range(2):
            for b in range(2):
                part = y[b][t * cols:(t + 1) * cols]
                acc[t, 0, b] += s0 * part
                acc[t, 1, b] += s1 * part
        return 0

    lax.fori_loop(0, 4, row_step, 0)
    for t in range(2):
        for a in range(2):
            for b in range(2):
                for lane in range(0, d, 128):
                    inter[lane // 128, pl.ds(b, cols, stride=2), :] = acc[t, a, b, :, lane:lane + 128]
            for lane in range(0, d, 128):
                out_ref[2 * t + a, :, lane:lane + 128] = inter[lane // 128].astype(BF)


def decode(canvas, proj, uup, bup, ulo, blo):
    cols, d = canvas.shape[1], proj.shape[1]
    return pl.pallas_call(
        functools.partial(decode_kernel, cols, d),
        out_shape=jax.ShapeDtypeStruct((4, 2 * cols, d), BF),
        in_specs=[VM, VM, HB, VM, HB, VM],
        out_specs=VM,
        scratch_shapes=[
            pltpu.VMEM((4, cols + 2 * PAD, d), F32),
            pltpu.VMEM((6, 2, cols + 2 * PAD, d), F32),
            pltpu.VMEM((2, 2, cols, d), F32),
            pltpu.VMEM((2, 2, 2, cols, d), F32),
            pltpu.VMEM((d // 128, 2 * cols, 128), F32),
            pltpu.VMEM((9, d, d), BF),
            pltpu.VMEM((16, d, d), BF),
            pltpu.SemaphoreType.DMA((9,)),
            pltpu.SemaphoreType.DMA((16,)),
        ],
        compiler_params=pltpu.CompilerParams(vmem_limit_bytes=60 * 2**20),
        name="decode",
    )(canvas, proj, uup, bup, ulo, blo)


def on_device(
    latent,
    tile_reach,
    first_weight,
    first_bias,
    second_weight,
    second_bias,
    proj_weight,
    upper_weight,
    upper_bias,
    lower_weight,
    lower_bias,
):
    chans = first_weight.shape[2]
    rows = latent.shape[0]
    cols = latent.shape[1] // chans
    core = latent.reshape(rows, cols, chans)
    lands = halo(core)
    y = tiles(tile_reach, core, lands, first_weight, first_bias[None], second_weight, second_bias[None])
    canvas, uup, ulo = blend(tile_reach, y, rows, cols, upper_weight, lower_weight)
    return decode(canvas, proj_weight, uup, upper_bias[None], ulo, lower_bias[None])


def solution(mesh):
    in_specs = (P("row", "col"), P(), P(), P(), P(), P(), P(), P(), P(), P(), P())
    out_specs = P(("row", "col"), None, None)
    return jax.shard_map(on_device, mesh=mesh, in_specs=in_specs, out_specs=out_specs, check_vma=False)
```

```python
import functools

import jax
import jax.numpy as jnp
from jax import lax
from jax.experimental import pallas as pl
from jax.experimental.pallas import tpu as pltpu
from jax.sharding import PartitionSpec as P

MARGIN = 4
SIDE = 8
PAD = 8
F32 = jnp.float32
BF = jnp.bfloat16
MESH = pl.DeviceIdType.MESH
VM = pl.BlockSpec(memory_space=pltpu.VMEM)
HB = pl.BlockSpec(memory_space=pltpu.HBM)
SM = pl.BlockSpec(memory_space=pltpu.SMEM)
AROUND = [(dr, dc) for dr in (-1, 0, 1) for dc in (-1, 0, 1) if (dr, dc) != (0, 0)]


def dot(a, b):
    return jnp.dot(a, b, preferred_element_type=F32)


def peer(row, col, dr, dc):
    rows, cols = lax.axis_size("row"), lax.axis_size("col")
    return lax.rem(row + (dr + rows), rows), lax.rem(col + (dc + cols), cols)


def place(reach_ref, row, col, dr, dc, rows, cols):
    n_row, n_col = lax.axis_size("row"), lax.axis_size("col")
    there = (row + dr >= 0) & (row + dr < n_row) & (col + dc >= 0) & (col + dc < n_col)
    r = lax.rem(row + (dr + n_row), n_row)
    c = lax.rem(col + (dc + n_col), n_col)
    low_r = jnp.maximum((row + dr) * rows - reach_ref[r, 0, c], 0)
    high_r = jnp.minimum((row + dr + 1) * rows + reach_ref[r, 1, c], rows * n_row)
    low_c = jnp.maximum((col + dc) * cols - reach_ref[r, 2, c], 0)
    high_c = jnp.minimum((col + dc + 1) * cols + reach_ref[r, 3, c], cols * n_col)
    return low_r, jnp.where(there, high_r, low_r), low_c, high_c


def spread(g):
    outer = 0.5 * (g[0] + g[2])
    mid = 0.5 * g[1]
    return [g[0], outer + mid, outer - mid, g[2]]


def upper_forms(up, out, sl, ln):
    cols = []
    for b in range(3):
        w = [up[a, b, sl, ln].astype(F32) for a in range(3)]
        cols.append([w[0], w[0] + w[1] + w[2], w[2]])
    for p in range(3):
        v = [cols[0][p], cols[0][p] + cols[1][p] + cols[2][p], cols[2][p]]
        for q in range(3):
            out[3 * p + q, sl, ln] = v[q].astype(BF)


def lower_forms(lo, out, sl, ln):
    cols = [spread([lo[a, b, sl, ln].astype(F32) for a in range(3)]) for b in range(3)]
    for r in range(4):
        v = spread([cols[b][r] for b in range(3)])
        for c in range(4):
            out[4 * r + c, sl, ln] = v[c].astype(BF)


def front_kernel(
    reach_ref, lat_ref, w1_hbm, b1_ref, w2_hbm, b2_ref, up_hbm, lo_hbm, out_ref, oux_ref, uo_hbm, vo_hbm, *refs
):
    lands, strips = refs[:8], refs[8:16]
    core_ref, side, side2, stage, x, act, ga, rest, w1, w2, r1, r2, y_ref, can, canx, count_ref, up, lo, uo, vo = refs[16:36]
    send0, recv0, send, recv, send2, recv2, sendx, recvx, self_sem, wsem, usem, vsem = refs[36:]
    rows, cols, ch = core_ref.shape
    m = MARGIN
    high, wide, span = rows + 2 * m, cols + 2 * SIDE, cols + 2 * m
    base = SIDE - m
    main = ch // 128 * 128
    left = ch - main
    part = 8
    row, col = lax.axis_index("row"), lax.axis_index("col")
    n_col = lax.axis_size("col")
    barrier = pltpu.get_barrier_semaphore()
    greet = [peer(row, col, 0, o) for o in range(1, n_col)]
    greet += [peer(row, col, dr, dc) for dr, dc in AROUND if dr != 0]
    for g in greet:
        pl.semaphore_signal(barrier, inc=1, device_id=g, device_id_type=MESH)
    loads = [
        pltpu.make_async_copy(src, dst, wsem.at[n])
        for n, (src, dst) in enumerate(((w1_hbm, w1), (w2_hbm, w2), (up_hbm, up), (lo_hbm, lo)))
    ]
    for c in loads[:2]:
        c.start()
    low_r, high_r, low_c, high_c = place(reach_ref, row, col, 0, 0, rows, cols)
    top, start = row * rows - m, col * cols - SIDE

    def put(dr, dc, at, num, value):
        lo_c, hi_c = {-1: (0, SIDE), 0: (SIDE, SIDE + cols), 1: (SIDE + cols, wide)}[dc]
        rid = lax.broadcasted_iota(jnp.int32, value.shape, 0) + (top + at)
        cid = lax.broadcasted_iota(jnp.int32, value.shape, 1) + (start + lo_c)
        ok = (rid >= low_r) & (rid < high_r) & (cid >= low_c) & (cid < high_c)
        x[pl.ds(at + 1, num), lo_c:hi_c] = jnp.where(ok, value.astype(F32), 0.0)

    def put_core(n, _):
        put(0, 0, m + part * n, part, core_ref[pl.ds(part * n, part)])
        return 0

    for c in range(cols):
        v = lat_ref[:, ch * c : ch * (c + 1)].astype(F32)
        for n in range(pl.cdiv(ch, 128)):
            size = min(128, ch - 128 * n)
            piece = v[:, 128 * n : 128 * n + size]
            if size < 128:
                piece = jnp.concatenate([piece, jnp.zeros((rows, 128 - size), F32)], axis=1)
            stage[n, pl.ds(c, rows, stride=cols), :] = piece
    for n in range(pl.cdiv(ch, 128)):
        size = min(128, ch - 128 * n)
        core_ref[:, :, 128 * n : 128 * n + size] = stage[n].reshape(rows, cols, 128)[:, :, :size].astype(BF)

    def turned(v):
        return jnp.concatenate([v[:, 4:8], v[:, 0:4]], axis=1)

    mid_row = rows // 2
    for n, at in ((0, cols - SIDE), (1, 0)):
        v = core_ref[:, at : at + SIDE].astype(F32)
        lo_half, hi_half = (turned(v[:mid_row]), v[mid_row:]) if n == 0 else (v[:mid_row], turned(v[mid_row:]))
        low_lanes = lax.broadcasted_iota(jnp.int32, lo_half.shape, 1) < m
        side[n] = jnp.where(low_lanes, lo_half, hi_half).astype(BF)
    pl.semaphore_wait(barrier, len(greet))
    halos = []
    for n, (dr, dc) in enumerate(AROUND):
        rs = {-1: pl.ds(rows - m, m), 0: pl.ds(0, rows), 1: pl.ds(0, m)}[dr]
        cs = {-1: pl.ds(cols - SIDE, SIDE), 0: pl.ds(0, cols), 1: pl.ds(0, SIDE)}[dc]
        halos.append(
            pltpu.make_async_remote_copy(
                src_ref=core_ref.at[rs, cs] if dr != 0 else side.at[0 if dc < 0 else 1],
                dst_ref=lands[n],
                send_sem=send0.at[n],
                recv_sem=recv0.at[n],
                device_id=peer(row, col, -dr, -dc),
                device_id_type=MESH,
            )
        )
        halos[-1].start()
    for c in loads[2:]:
        c.start()
    lax.fori_loop(0, rows // part, put_core, 0)
    for buf in (x, act):
        buf[0] = jnp.zeros((wide, ch), F32)
        buf[high + 1] = jnp.zeros((wide, ch), F32)

    def clear(n, _):
        act[pl.ds(part * n + 1, part), 0:8, :] = jnp.zeros((part, 8, ch), F32)
        act[pl.ds(part * n + 1, part), wide - 8 : wide, :] = jnp.zeros((part, 8, ch), F32)
        return 0

    lax.fori_loop(0, high // part, clear, 0)
    shape = count_ref.shape
    rid = lax.broadcasted_iota(jnp.int32, shape, 0) + (row * rows - 1)
    cid = lax.broadcasted_iota(jnp.int32, shape, 1) + col * cols
    total = jnp.zeros(shape, F32)
    for dr in (-1, 0, 1):
        for dc in (-1, 0, 1):
            lr, hr, lc, hc = place(reach_ref, row, col, dr, dc, rows, cols)
            inside = (rid >= lr) & (rid < hr) & (cid >= lc) & (cid < hc)
            total += jnp.where(inside, 1.0, 0.0)
    count_ref[...] = total

    def narrow(w, r):
        r[...] = jnp.concatenate([w[dr, :, main:] for dr in range(3)], axis=1)

    for c in loads[:2]:
        c.wait()
    narrow(w1, r1)
    narrow(w2, r2)
    for c in halos:
        c.wait()
    got = dict(zip(AROUND, lands))
    for dr, dc in AROUND:
        if dr == 0:

            def put_side(n, _):
                v = got[0, dc][pl.ds(part * n, part)].astype(F32)
                pair = (turned(v), v) if dc < 0 else (v, turned(v))
                put(0, dc, m + part * n, part, pair[0])
                put(0, dc, m + mid_row + part * n, part, pair[1])
                return 0

            lax.fori_loop(0, mid_row // part, put_side, 0)
        else:
            put(dr, dc, 0 if dr < 0 else m + rows, m, got[dr, dc][...])

    def gather(buf):
        def group(n, _):
            for k in range(3):
                at = 6 * n + 2 * k
                pieces = [
                    buf[pl.ds(at, 2), base + dc : base + dc + span, :].reshape(2 * span, ch) for dc in (-1, 0, 1)
                ]
                v = jnp.concatenate(pieces, axis=1).astype(BF)
                ga[pl.ds(pl.multiple_of(span * at, 16), 2 * span), :] = v
            return 0

        lax.fori_loop(0, (high + 2) // 6, group, 0)

    half = high // 2
    count = half * span

    def conv(w, r, b_ref, finish):
        for n in range(2):
            size = (high + 2) // 2 * span
            rest[pl.ds(n * size, size), :] = dot(ga[pl.ds(n * size, size), :], r[...])

        for n in range(2):
            at = n * count
            big = (
                dot(ga[pl.ds(at, count), :], w[0, :, :main])
                + dot(ga[pl.ds(at + span, count), :], w[1, :, :main])
                + dot(ga[pl.ds(at + 2 * span, count), :], w[2, :, :main])
            )
            finish(n, 0, main, big + b_ref[:main][None])
            small = (
                rest[pl.ds(at, count), :left]
                + rest[pl.ds(at + span, count), left : 2 * left]
                + rest[pl.ds(at + 2 * span, count), 2 * left :]
            )
            finish(n, main, ch, small + b_ref[main:][None])

    def window_mask(n, width):
        rid = lax.broadcasted_iota(jnp.int32, (half, 1, width), 0) + (top + n * half)
        kid = lax.broadcasted_iota(jnp.int32, (1, span, width), 1) + (start + base)
        row_one = jnp.where((rid >= low_r) & (rid < high_r), 1.0, 0.0)
        col_one = jnp.where((kid >= low_c) & (kid < high_c), 1.0, 0.0)
        return row_one * col_one

    def first(n, lo, hi, v):
        v = 0.5 * v
        v = (v + v * jnp.tanh(v)).reshape(half, span, hi - lo)
        act[pl.ds(n * half + 1, half), base : base + span, lo:hi] = v * window_mask(n, hi - lo)

    def second(n, lo, hi, v):
        here = pl.ds(n * half + 1, half)
        v = v.reshape(half, span, hi - lo) + x[here, base : base + span, lo:hi]
        act[here, base : base + span, lo:hi] = v * window_mask(n, hi - lo)

    gather(x)
    conv(w1, r1, b1_ref, first)
    gather(act)
    conv(w2, r2, b2_ref, second)

    def emit(n, _):
        y_ref[pl.ds(part * n, part)] = act[pl.ds(part * n + 1, part)].astype(BF)
        return 0

    lax.fori_loop(0, high // part, emit, 0)
    edge = m + 1
    tall = rows + 2
    cut = tall // 2
    for n, at in ((0, SIDE + cols), (1, 0)):
        v = act[pl.ds(m, cut), at : at + SIDE] + turned(act[pl.ds(m + cut, cut), at : at + SIDE])
        side2[n] = v.astype(BF)
    copies = []
    for n, (dr, dc) in enumerate(AROUND):
        rs = {-1: pl.ds(high - edge, edge), 0: pl.ds(m - 1, tall), 1: pl.ds(0, edge)}[dr]
        cs = {-1: pl.ds(SIDE + cols, SIDE), 0: pl.ds(SIDE, cols), 1: pl.ds(0, SIDE)}[dc]
        copies.append(
            pltpu.make_async_remote_copy(
                src_ref=y_ref.at[rs, cs] if dr != 0 else side2.at[0 if dc < 0 else 1],
                dst_ref=strips[n],
                send_sem=send.at[n],
                recv_sem=recv.at[n],
                device_id=peer(row, col, -dr, -dc),
                device_id_type=MESH,
            )
        )
        copies[-1].start()
    depth, width = up.shape[2:]
    block = 64
    stores = []

    def forms(form, src, dst, dst_hbm, sem):
        def store(n):
            sl = pl.ds(pl.multiple_of(n * block, block), block)
            return pltpu.make_async_copy(dst.at[:, sl], dst_hbm.at[:, sl], sem.at[n])

        def body(n, _):
            def inner(k, _):
                sl = pl.ds(pl.multiple_of(n * block + k * 16, 16), 16)
                for lane in range(0, width, 128):
                    form(src, dst, sl, slice(lane, lane + 128))
                return 0

            lax.fori_loop(0, block // 16, inner, 0)
            store(n).start()
            return 0

        lax.fori_loop(0, depth // block, body, 0)
        stores.extend(store(n) for n in range(depth // block))

    loads[2].wait()
    forms(upper_forms, up, uo, uo_hbm, usem)
    for c in copies:
        c.wait()
    got2 = dict(zip(AROUND, strips))

    main = 256

    def merge(lo_r, num, dr):
        here = pl.ds(lo_r, num)
        total = y_ref[pl.ds(m - 1 + lo_r, num), SIDE : SIDE + cols].astype(F32)
        late = lo_r >= cut
        there = pl.ds(lo_r - cut if late else lo_r, num)
        lhs, rhs = got2[0, -1][there].astype(F32), got2[0, 1][there].astype(F32)
        if late:
            lhs, rhs = turned(lhs), turned(rhs)
        low = lax.broadcasted_iota(jnp.int32, lhs.shape, 1) < m
        lhs, rhs = jnp.where(low, lhs, 0.0), jnp.where(low, 0.0, rhs)
        if dr:
            total += got2[dr, 0][...].astype(F32)
            lhs += got2[dr, -1][...].astype(F32)
            rhs += got2[dr, 1][...].astype(F32)
        total += jnp.concatenate([lhs, rhs], axis=1)
        n = count_ref[here][:, :, :1]
        total = jnp.where(n > 0, total / jnp.maximum(n, 1.0), 0.0)
        can[here] = total[:, :, :main].astype(BF)
        canx[here] = jnp.concatenate([total[:, :8, main:], total[:, 8:, main:]], axis=2).astype(BF)

    merge(0, edge, -1)
    merge(edge, cut - edge, 0)
    merge(cut, cut - edge, 0)
    merge(tall - edge, edge, 1)
    mine = pl.ds(pl.multiple_of(cols * col, cols), cols)
    step = rows // n_col
    deep = step + 2
    minex = pl.ds(pl.multiple_of(8 * col, 8), 8)
    own = [
        pltpu.make_async_copy(can.at[pl.ds(step * col, deep)], out_ref.at[:, mine], self_sem.at[0]),
        pltpu.make_async_copy(canx.at[pl.ds(step * col, deep)], oux_ref.at[:, minex], self_sem.at[1]),
    ]
    for c in own:
        c.start()

    def send_rows(to, at, spot, spotx, o):
        return [
            pltpu.make_async_remote_copy(
                src_ref=src.at[pl.ds(at, deep)],
                dst_ref=dst.at[:, where],
                send_sem=ss.at[o],
                recv_sem=rs.at[o],
                device_id=to,
                device_id_type=MESH,
            )
            for src, dst, where, ss, rs in (
                (can, out_ref, spot, send2, recv2),
                (canx, oux_ref, spotx, sendx, recvx),
            )
        ]

    copies = []
    for o in range(1, n_col):
        to = peer(row, col, 0, o)
        copies.append(send_rows(to, step * to[1], mine, minex, o))
        for c in copies[-1]:
            c.start()
    loads[3].wait()
    forms(lower_forms, lo, vo, vo_hbm, vsem)
    for c in stores:
        c.wait()
    for c in own:
        c.wait()
    for o in range(1, n_col):
        src = peer(row, col, 0, -o)
        spot = pl.ds(pl.multiple_of(cols * src[1], cols), cols)
        spotx = pl.ds(pl.multiple_of(8 * src[1], 8), 8)
        for c in copies[o - 1]:
            c.wait_send()
        for c in send_rows(src, 0, spot, spotx, o):
            c.wait_recv()


def front(reach, latent, w1, b1, w2, b2, upper, lower):
    ch = w1.shape[2]
    rows, cols = latent.shape[0], latent.shape[1] // ch
    d = upper.shape[2]
    m = MARGIN
    high, wide, span = rows + 2 * m, cols + 2 * SIDE, cols + 2 * m
    n_col = lax.axis_size("col")
    tall = rows + 2
    deep = rows // n_col + 2
    left = 3 * (ch % 128)
    w1, w2 = (w.reshape(3, 3 * ch, ch) for w in (w1, w2))

    def around(full, thin):
        return [pltpu.VMEM((full // 2 if dr == 0 else thin, cols if dc == 0 else SIDE, ch), BF) for dr, dc in AROUND]

    return pl.pallas_call(
        front_kernel,
        out_shape=[
            jax.ShapeDtypeStruct((deep, n_col * cols, 256), BF),
            jax.ShapeDtypeStruct((deep, n_col * 8, 128), BF),
            jax.ShapeDtypeStruct((9, d, d), BF),
            jax.ShapeDtypeStruct((16, d, d), BF),
        ],
        in_specs=[SM, VM, HB, VM, HB, VM, HB, HB],
        out_specs=[VM, VM, HB, HB],
        scratch_shapes=around(rows, m)
        + around(tall, m + 1)
        + [
            pltpu.VMEM((rows, cols, ch), BF),
            pltpu.VMEM((2, rows // 2, SIDE, ch), BF),
            pltpu.VMEM((2, tall // 2, SIDE, ch), BF),
            pltpu.VMEM((pl.cdiv(ch, 128), rows * cols, 128), F32),
            pltpu.VMEM((high + 2, wide, ch), F32),
            pltpu.VMEM((high + 2, wide, ch), F32),
            pltpu.VMEM(((high + 2) * span, 3 * ch), BF),
            pltpu.VMEM(((high + 2) * span, left), F32),
            pltpu.VMEM((3, 3 * ch, ch), BF),
            pltpu.VMEM((3, 3 * ch, ch), BF),
            pltpu.VMEM((3 * ch, left), BF),
            pltpu.VMEM((3 * ch, left), BF),
            pltpu.VMEM((high, wide, ch), BF),
            pltpu.VMEM((tall, cols, 256), BF),
            pltpu.VMEM((tall, 8, 128), BF),
            pltpu.VMEM((tall, cols, 128), F32),
            pltpu.VMEM((3, 3, d, d), BF),
            pltpu.VMEM((3, 3, d, d), BF),
            pltpu.VMEM((9, d, d), BF),
            pltpu.VMEM((16, d, d), BF),
        ]
        + [pltpu.SemaphoreType.DMA((8,))] * 4
        + [
            pltpu.SemaphoreType.DMA((n_col,)),
            pltpu.SemaphoreType.DMA((n_col,)),
            pltpu.SemaphoreType.DMA((n_col,)),
            pltpu.SemaphoreType.DMA((n_col,)),
            pltpu.SemaphoreType.DMA((2,)),
            pltpu.SemaphoreType.DMA((4,)),
            pltpu.SemaphoreType.DMA((d // 64,)),
            pltpu.SemaphoreType.DMA((d // 64,)),
        ],
        compiler_params=pltpu.CompilerParams(
            collective_id=0, has_side_effects=True, vmem_limit_bytes=60 * 2**20
        ),
        name="front",
    )(reach, latent, w1, b1, w2, b2, upper, lower)


def decode_kernel(cols, d, can_ref, canx_ref, proj_ref, uup_hbm, bup_ref, ulo_hbm, blo_ref, out_ref,
                  hid, act, ts, acc, inter, projx, obuf, uup, ulo, upsem, losem, osem):
    row, col = lax.axis_index("row"), lax.axis_index("col")
    first_dev = (row == 0) & (col == 0)
    last_dev = (row == lax.axis_size("row") - 1) & (col == lax.axis_size("col") - 1)
    upc = [pltpu.make_async_copy(uup_hbm.at[i], uup.at[i], upsem.at[i]) for i in range(9)]
    loc = [pltpu.make_async_copy(ulo_hbm.at[i], ulo.at[i], losem.at[i]) for i in range(16)]
    for i in (3, 4, 5, 6, 7, 8, 0, 1, 2):
        upc[i].start()
    for c in loc:
        c.start()
    body = pl.ds(PAD, cols)
    prev = pl.ds(PAD - 1, cols)
    nxt = pl.ds(PAD + 1, cols)
    zero8 = jnp.zeros((4, PAD, d), F32)
    hid[:, 0:PAD, :] = zero8
    hid[:, PAD + cols:, :] = zero8
    zact = jnp.zeros((6, 2, PAD, d), F32)
    act[:, :, 0:PAD, :] = zact
    act[:, :, PAD + cols:, :] = zact
    rest = proj_ref[256:]
    blank = jnp.zeros((64, d), BF)
    projx[0:64, 0:d] = rest
    projx[0:64, d : 2 * d] = blank
    projx[64:128, 0:d] = blank
    projx[64:128, d : 2 * d] = rest
    for i in range(4):
        extra = dot(canx_ref[i], projx[...])
        extra = jnp.concatenate(
            [extra[:, :d].reshape(cols // 16, 8, d), extra[:, d:].reshape(cols // 16, 8, d)], axis=1
        ).reshape(cols, d)
        v = (dot(can_ref[i], proj_ref[0:256]) + extra).astype(BF).astype(F32)
        hid[i, body, :] = v

    def three(load):
        mid = load(body)
        return [(load(prev) - mid).astype(BF), mid.astype(BF), (load(nxt) - mid).astype(BF)]

    def both(x, p):
        s = dot(x[1], uup[3 * p + 1])
        return s + dot(x[0], uup[3 * p]), s + dot(x[2], uup[3 * p + 2])

    def middle(k):
        e, o = both(three(lambda sl: hid[k, sl, :]), 1)
        ts[k % 2, 0] = e + bup_ref[...]
        ts[k % 2, 1] = o + bup_ref[...]

    def act_row(slot, par, v):
        half = 0.5 * v
        act[slot, par, body, :] = half + half * jnp.tanh(half)

    for i in (3, 4, 5):
        upc[i].wait()
    middle(0)
    for i in (6, 7, 8, 0, 1, 2):
        upc[i].wait()

    def step(k, _):
        x = three(lambda sl: hid[k + 1, sl, :] - hid[k, sl, :])
        down = both(x, 2)
        for par in range(2):
            act_row(2 * k, par, ts[k % 2, par] + down[par])
        middle(k + 1)
        up = both(x, 0)
        for par in range(2):
            act_row(2 * k + 1, par, ts[(k + 1) % 2, par] - up[par])
        return 0

    lax.fori_loop(0, 3, step, 0)

    @pl.when(first_dev)
    def _():
        act[0, :, body, :] = jnp.zeros((2, cols, d), F32)

    @pl.when(last_dev)
    def _():
        act[5, :, body, :] = jnp.zeros((2, cols, d), F32)

    for c in loc:
        c.wait()

    def products(r):
        one, two, sgn = ((0, 2, -1), (1, 2, 1), (2, 1, -1), (1, 3, -1))[r]
        vs = [[], [], [], []]
        for t in range(2):

            def ld(par, sl):
                u, v = act[2 * t + one, par, sl, :], act[2 * t + two, par, sl, :]
                return u + v if sgn > 0 else u - v

            ev = ld(0, body)
            od = ld(1, body)
            vs[0].append((ld(1, prev) - od).astype(BF))
            vs[1].append((ev + od).astype(BF))
            vs[2].append((od - ev).astype(BF))
            vs[3].append((ev - ld(0, nxt)).astype(BF))
        m = [dot(jnp.concatenate(vs[c], axis=0), ulo[4 * r + c]) for c in range(4)]
        plus, minus = m[1] + m[2], m[1] - m[2]
        y = [plus + m[0], minus - m[3]]
        return [[y[b][t * cols : (t + 1) * cols] for b in range(2)] for t in range(2)]

    ocp = [pltpu.make_async_copy(obuf.at[i], out_ref.at[i], osem.at[i]) for i in range(4)]

    def emit(t, a, b, v):
        for lane in range(0, d, 128):
            inter[2 * t + a, lane // 128, pl.ds(b, cols, stride=2), :] = v[:, lane : lane + 128]

    def flush(a):
        for t in range(2):
            for lane in range(0, d, 128):
                obuf[2 * t + a, :, lane : lane + 128] = inter[2 * t + a, lane // 128].astype(BF)
            ocp[2 * t + a].start()

    def inner_pair(_, carry):
        y = products(1)
        for t in range(2):
            h = hid[t + 1, body, :] + blo_ref[...]
            for b in range(2):
                v = h + y[t][b]
                acc[t, 0, b] = v
                acc[t, 1, b] = v
        y = products(2)
        for t in range(2):
            for b in range(2):
                acc[t, 0, b] += y[t][b]
                acc[t, 1, b] -= y[t][b]
        return carry

    def outer_pair(_, carry):
        y = products(0)
        for t in range(2):
            for b in range(2):
                emit(t, 0, b, acc[t, 0, b] + y[t][b])
        flush(0)
        y = products(3)
        for t in range(2):
            for b in range(2):
                emit(t, 1, b, acc[t, 1, b] - y[t][b])
        flush(1)
        return carry

    once = 1 + row // lax.axis_size("row")
    lax.fori_loop(0, once, inner_pair, 0)
    outer_pair(0, 0)
    for c in ocp:
        c.wait()


def decode(canvas, extra, proj, uup, bup, ulo, blo):
    cols, d = canvas.shape[1], proj.shape[1]
    return pl.pallas_call(
        functools.partial(decode_kernel, cols, d),
        out_shape=jax.ShapeDtypeStruct((4, 2 * cols, d), BF),
        in_specs=[VM, VM, VM, HB, VM, HB, VM],
        out_specs=HB,
        scratch_shapes=[
            pltpu.VMEM((4, cols + 2 * PAD, d), F32),
            pltpu.VMEM((6, 2, cols + 2 * PAD, d), F32),
            pltpu.VMEM((2, 2, cols, d), F32),
            pltpu.VMEM((2, 2, 2, cols, d), F32),
            pltpu.VMEM((4, d // 128, 2 * cols, 128), F32),
            pltpu.VMEM((128, 2 * d), BF),
            pltpu.VMEM((4, 2 * cols, d), BF),
            pltpu.VMEM((9, d, d), BF),
            pltpu.VMEM((16, d, d), BF),
            pltpu.SemaphoreType.DMA((9,)),
            pltpu.SemaphoreType.DMA((16,)),
            pltpu.SemaphoreType.DMA((4,)),
        ],
        compiler_params=pltpu.CompilerParams(vmem_limit_bytes=60 * 2**20),
        name="decode",
    )(canvas, extra, proj, uup, bup, ulo, blo)


def on_device(
    latent,
    tile_reach,
    first_weight,
    first_bias,
    second_weight,
    second_bias,
    proj_weight,
    upper_weight,
    upper_bias,
    lower_weight,
    lower_bias,
):
    canvas, extra, uup, ulo = front(
        tile_reach.transpose(0, 2, 1),
        latent,
        first_weight,
        first_bias,
        second_weight,
        second_bias,
        upper_weight,
        lower_weight,
    )
    return decode(canvas, extra, proj_weight, uup, upper_bias[None], ulo, lower_bias[None])


def solution(mesh):
    in_specs = (P("row", "col"), P(), P(), P(), P(), P(), P(), P(), P(), P(), P())
    out_specs = P(("row", "col"), None, None)
    return jax.shard_map(on_device, mesh=mesh, in_specs=in_specs, out_specs=out_specs, check_vma=False)
```

```python
import functools

import jax
import jax.numpy as jnp
from jax import lax
from jax.experimental import pallas as pl
from jax.experimental.pallas import tpu as pltpu
from jax.sharding import PartitionSpec as P

MARGIN = 4
SIDE = 8
PAD = 8
F32 = jnp.float32
BF = jnp.bfloat16
MESH = pl.DeviceIdType.MESH
VM = pl.BlockSpec(memory_space=pltpu.VMEM)
HB = pl.BlockSpec(memory_space=pltpu.HBM)
SM = pl.BlockSpec(memory_space=pltpu.SMEM)
AROUND = [(dr, dc) for dr in (-1, 0, 1) for dc in (-1, 0, 1) if (dr, dc) != (0, 0)]


def dot(a, b):
    return jnp.dot(a, b, preferred_element_type=F32)


def peer(row, col, dr, dc):
    rows, cols = lax.axis_size("row"), lax.axis_size("col")
    return lax.rem(row + (dr + rows), rows), lax.rem(col + (dc + cols), cols)


def place(reach_ref, row, col, dr, dc, rows, cols):
    n_row, n_col = lax.axis_size("row"), lax.axis_size("col")
    there = (row + dr >= 0) & (row + dr < n_row) & (col + dc >= 0) & (col + dc < n_col)
    r = lax.rem(row + (dr + n_row), n_row)
    c = lax.rem(col + (dc + n_col), n_col)
    low_r = jnp.maximum((row + dr) * rows - reach_ref[r, 0, c], 0)
    high_r = jnp.minimum((row + dr + 1) * rows + reach_ref[r, 1, c], rows * n_row)
    low_c = jnp.maximum((col + dc) * cols - reach_ref[r, 2, c], 0)
    high_c = jnp.minimum((col + dc + 1) * cols + reach_ref[r, 3, c], cols * n_col)
    return low_r, jnp.where(there, high_r, low_r), low_c, high_c


def spread(g):
    outer = 0.5 * (g[0] + g[2])
    mid = 0.5 * g[1]
    return [g[0], outer + mid, outer - mid, g[2]]


def upper_forms(up, out, sl, ln):
    cols = []
    for b in range(3):
        w = [up[a, b, sl, ln].astype(F32) for a in range(3)]
        cols.append([w[0], w[0] + w[1] + w[2], w[2]])
    for p in range(3):
        v = [cols[0][p], cols[0][p] + cols[1][p] + cols[2][p], cols[2][p]]
        for q in range(3):
            out[3 * p + q, sl, ln] = v[q].astype(BF)


def lower_forms(lo, out, sl, ln):
    cols = [spread([lo[a, b, sl, ln].astype(F32) for a in range(3)]) for b in range(3)]
    for r in range(4):
        v = spread([cols[b][r] for b in range(3)])
        for c in range(4):
            out[4 * r + c, sl, ln] = v[c].astype(BF)


def front_kernel(
    reach_ref, lat_ref, w1_hbm, b1_ref, w2_hbm, b2_ref, up_hbm, lo_hbm, out_ref, oux_ref, uo_hbm, vo_hbm, *refs
):
    lands, strips = refs[:8], refs[8:16]
    core_ref, side, side2, stage, x, act, ga, rest, w1, w2, r1, r2, y_ref, can, canx, count_ref, up, lo, uo, vo = refs[16:36]
    send0, recv0, send, recv, send2, recv2, sendx, recvx, self_sem, wsem, usem, vsem = refs[36:]
    rows, cols, ch = core_ref.shape
    m = MARGIN
    high, wide, span = rows + 2 * m, cols + 2 * SIDE, cols + 2 * m
    base = SIDE - m
    main = ch // 128 * 128
    left = ch - main
    part = 8
    row, col = lax.axis_index("row"), lax.axis_index("col")
    n_col = lax.axis_size("col")
    barrier = pltpu.get_barrier_semaphore()
    greet = [peer(row, col, 0, o) for o in range(1, n_col)]
    greet += [peer(row, col, dr, dc) for dr, dc in AROUND if dr != 0]
    for g in greet:
        pl.semaphore_signal(barrier, inc=1, device_id=g, device_id_type=MESH)
    loads = [
        pltpu.make_async_copy(src, dst, wsem.at[n])
        for n, (src, dst) in enumerate(((w1_hbm, w1), (w2_hbm, w2), (up_hbm, up), (lo_hbm, lo)))
    ]
    for c in loads[:2]:
        c.start()
    low_r, high_r, low_c, high_c = place(reach_ref, row, col, 0, 0, rows, cols)
    top, start = row * rows - m, col * cols - SIDE

    def put(dr, dc, at, num, value):
        lo_c, hi_c = {-1: (0, SIDE), 0: (SIDE, SIDE + cols), 1: (SIDE + cols, wide)}[dc]
        rid = lax.broadcasted_iota(jnp.int32, value.shape, 0) + (top + at)
        cid = lax.broadcasted_iota(jnp.int32, value.shape, 1) + (start + lo_c)
        ok = (rid >= low_r) & (rid < high_r) & (cid >= low_c) & (cid < high_c)
        x[pl.ds(at + 1, num), lo_c:hi_c] = jnp.where(ok, value.astype(F32), 0.0)

    def put_core(n, _):
        put(0, 0, m + part * n, part, core_ref[pl.ds(part * n, part)])
        return 0

    for c in range(cols):
        v = lat_ref[:, ch * c : ch * (c + 1)].astype(F32)
        for n in range(pl.cdiv(ch, 128)):
            size = min(128, ch - 128 * n)
            piece = v[:, 128 * n : 128 * n + size]
            if size < 128:
                piece = jnp.concatenate([piece, jnp.zeros((rows, 128 - size), F32)], axis=1)
            stage[n, pl.ds(c, rows, stride=cols), :] = piece
    for n in range(pl.cdiv(ch, 128)):
        size = min(128, ch - 128 * n)
        core_ref[:, :, 128 * n : 128 * n + size] = stage[n].reshape(rows, cols, 128)[:, :, :size].astype(BF)

    def turned(v):
        return jnp.concatenate([v[:, 4:8], v[:, 0:4]], axis=1)

    mid_row = rows // 2
    for n, at in ((0, cols - SIDE), (1, 0)):
        v = core_ref[:, at : at + SIDE].astype(F32)
        lo_half, hi_half = (turned(v[:mid_row]), v[mid_row:]) if n == 0 else (v[:mid_row], turned(v[mid_row:]))
        low_lanes = lax.broadcasted_iota(jnp.int32, lo_half.shape, 1) < m
        side[n] = jnp.where(low_lanes, lo_half, hi_half).astype(BF)
    pl.semaphore_wait(barrier, len(greet))
    halos = []
    for n, (dr, dc) in enumerate(AROUND):
        rs = {-1: pl.ds(rows - m, m), 0: pl.ds(0, rows), 1: pl.ds(0, m)}[dr]
        cs = {-1: pl.ds(cols - SIDE, SIDE), 0: pl.ds(0, cols), 1: pl.ds(0, SIDE)}[dc]
        halos.append(
            pltpu.make_async_remote_copy(
                src_ref=core_ref.at[rs, cs] if dr != 0 else side.at[0 if dc < 0 else 1],
                dst_ref=lands[n],
                send_sem=send0.at[n],
                recv_sem=recv0.at[n],
                device_id=peer(row, col, -dr, -dc),
                device_id_type=MESH,
            )
        )
        halos[-1].start()
    for c in loads[2:]:
        c.start()
    lax.fori_loop(0, rows // part, put_core, 0)
    for buf in (x, act):
        buf[0] = jnp.zeros((wide, ch), F32)
        buf[high + 1] = jnp.zeros((wide, ch), F32)

    def clear(n, _):
        act[pl.ds(part * n + 1, part), 0:8, :] = jnp.zeros((part, 8, ch), F32)
        act[pl.ds(part * n + 1, part), wide - 8 : wide, :] = jnp.zeros((part, 8, ch), F32)
        return 0

    lax.fori_loop(0, high // part, clear, 0)
    shape = count_ref.shape
    rid = lax.broadcasted_iota(jnp.int32, shape, 0) + (row * rows - 1)
    cid = lax.broadcasted_iota(jnp.int32, shape, 1) + col * cols
    total = jnp.zeros(shape, F32)
    for dr in (-1, 0, 1):
        for dc in (-1, 0, 1):
            lr, hr, lc, hc = place(reach_ref, row, col, dr, dc, rows, cols)
            inside = (rid >= lr) & (rid < hr) & (cid >= lc) & (cid < hc)
            total += jnp.where(inside, 1.0, 0.0)
    count_ref[...] = total

    def narrow(w, r):
        r[...] = jnp.concatenate([w[dr, :, main:] for dr in range(3)], axis=1)

    for c in loads[:2]:
        c.wait()
    narrow(w1, r1)
    narrow(w2, r2)
    for c in halos:
        c.wait()
    got = dict(zip(AROUND, lands))
    for dr, dc in AROUND:
        if dr == 0:

            def put_side(n, _):
                v = got[0, dc][pl.ds(part * n, part)].astype(F32)
                pair = (turned(v), v) if dc < 0 else (v, turned(v))
                put(0, dc, m + part * n, part, pair[0])
                put(0, dc, m + mid_row + part * n, part, pair[1])
                return 0

            lax.fori_loop(0, mid_row // part, put_side, 0)
        else:
            put(dr, dc, 0 if dr < 0 else m + rows, m, got[dr, dc][...])

    def gather(buf):
        def group(n, _):
            for k in range(3):
                at = 6 * n + 2 * k
                pieces = [
                    buf[pl.ds(at, 2), base + dc : base + dc + span, :].reshape(2 * span, ch) for dc in (-1, 0, 1)
                ]
                v = jnp.concatenate(pieces, axis=1).astype(BF)
                ga[pl.ds(pl.multiple_of(span * at, 16), 2 * span), :] = v
            return 0

        lax.fori_loop(0, (high + 2) // 6, group, 0)

    half = high // 2
    count = half * span

    def conv(w, r, b_ref, finish):
        for n in range(2):
            size = (high + 2) // 2 * span
            rest[pl.ds(n * size, size), :] = dot(ga[pl.ds(n * size, size), :], r[...])

        for n in range(2):
            at = n * count
            big = (
                dot(ga[pl.ds(at, count), :], w[0, :, :main])
                + dot(ga[pl.ds(at + span, count), :], w[1, :, :main])
                + dot(ga[pl.ds(at + 2 * span, count), :], w[2, :, :main])
            )
            finish(n, 0, main, big + b_ref[:main][None])
            small = (
                rest[pl.ds(at, count), :left]
                + rest[pl.ds(at + span, count), left : 2 * left]
                + rest[pl.ds(at + 2 * span, count), 2 * left :]
            )
            finish(n, main, ch, small + b_ref[main:][None])

    def window_mask(n, width):
        rid = lax.broadcasted_iota(jnp.int32, (half, 1, width), 0) + (top + n * half)
        kid = lax.broadcasted_iota(jnp.int32, (1, span, width), 1) + (start + base)
        row_one = jnp.where((rid >= low_r) & (rid < high_r), 1.0, 0.0)
        col_one = jnp.where((kid >= low_c) & (kid < high_c), 1.0, 0.0)
        return row_one * col_one

    def first(n, lo, hi, v):
        v = 0.5 * v
        v = (v + v * jnp.tanh(v)).reshape(half, span, hi - lo)
        act[pl.ds(n * half + 1, half), base : base + span, lo:hi] = v * window_mask(n, hi - lo)

    def second(n, lo, hi, v):
        here = pl.ds(n * half + 1, half)
        v = v.reshape(half, span, hi - lo) + x[here, base : base + span, lo:hi]
        act[here, base : base + span, lo:hi] = v * window_mask(n, hi - lo)

    gather(x)
    conv(w1, r1, b1_ref, first)
    gather(act)
    conv(w2, r2, b2_ref, second)

    def emit(n, _):
        y_ref[pl.ds(part * n, part)] = act[pl.ds(part * n + 1, part)].astype(BF)
        return 0

    lax.fori_loop(0, high // part, emit, 0)
    edge = m + 1
    tall = rows + 2
    cut = tall // 2
    for n, at in ((0, SIDE + cols), (1, 0)):
        v = act[pl.ds(m, cut), at : at + SIDE] + turned(act[pl.ds(m + cut, cut), at : at + SIDE])
        side2[n] = v.astype(BF)
    copies = []
    for n, (dr, dc) in enumerate(AROUND):
        rs = {-1: pl.ds(high - edge, edge), 0: pl.ds(m - 1, tall), 1: pl.ds(0, edge)}[dr]
        cs = {-1: pl.ds(SIDE + cols, SIDE), 0: pl.ds(SIDE, cols), 1: pl.ds(0, SIDE)}[dc]
        copies.append(
            pltpu.make_async_remote_copy(
                src_ref=y_ref.at[rs, cs] if dr != 0 else side2.at[0 if dc < 0 else 1],
                dst_ref=strips[n],
                send_sem=send.at[n],
                recv_sem=recv.at[n],
                device_id=peer(row, col, -dr, -dc),
                device_id_type=MESH,
            )
        )
        copies[-1].start()
    depth, width = up.shape[2:]
    block = 64
    stores = []

    def forms(form, src, dst, dst_hbm, sem):
        def store(n):
            sl = pl.ds(pl.multiple_of(n * block, block), block)
            return pltpu.make_async_copy(dst.at[:, sl], dst_hbm.at[:, sl], sem.at[n])

        def body(n, _):
            def inner(k, _):
                sl = pl.ds(pl.multiple_of(n * block + k * 16, 16), 16)
                for lane in range(0, width, 128):
                    form(src, dst, sl, slice(lane, lane + 128))
                return 0

            lax.fori_loop(0, block // 16, inner, 0)
            store(n).start()
            return 0

        lax.fori_loop(0, depth // block, body, 0)
        stores.extend(store(n) for n in range(depth // block))

    loads[2].wait()
    forms(upper_forms, up, uo, uo_hbm, usem)
    for c in copies:
        c.wait()
    got2 = dict(zip(AROUND, strips))

    main = 256

    def merge(lo_r, num, dr):
        here = pl.ds(lo_r, num)
        total = y_ref[pl.ds(m - 1 + lo_r, num), SIDE : SIDE + cols].astype(F32)
        late = lo_r >= cut
        there = pl.ds(lo_r - cut if late else lo_r, num)
        lhs, rhs = got2[0, -1][there].astype(F32), got2[0, 1][there].astype(F32)
        if late:
            lhs, rhs = turned(lhs), turned(rhs)
        low = lax.broadcasted_iota(jnp.int32, lhs.shape, 1) < m
        lhs, rhs = jnp.where(low, lhs, 0.0), jnp.where(low, 0.0, rhs)
        if dr:
            total += got2[dr, 0][...].astype(F32)
            lhs += got2[dr, -1][...].astype(F32)
            rhs += got2[dr, 1][...].astype(F32)
        total += jnp.concatenate([lhs, rhs], axis=1)
        n = count_ref[here][:, :, :1]
        total = jnp.where(n > 0, total / jnp.maximum(n, 1.0), 0.0)
        can[here] = total[:, :, :main].astype(BF)
        canx[here] = jnp.concatenate([total[:, :8, main:], total[:, 8:, main:]], axis=2).astype(BF)

    merge(0, edge, -1)
    merge(edge, cut - edge, 0)
    merge(cut, cut - edge, 0)
    merge(tall - edge, edge, 1)
    mine = pl.ds(pl.multiple_of(cols * col, cols), cols)
    step = rows // n_col
    deep = step + 2
    minex = pl.ds(pl.multiple_of(8 * col, 8), 8)
    own = [
        pltpu.make_async_copy(can.at[pl.ds(step * col, deep)], out_ref.at[:, mine], self_sem.at[0]),
        pltpu.make_async_copy(canx.at[pl.ds(step * col, deep)], oux_ref.at[:, minex], self_sem.at[1]),
    ]
    for c in own:
        c.start()

    def send_rows(to, at, spot, spotx, o):
        return [
            pltpu.make_async_remote_copy(
                src_ref=src.at[pl.ds(at, deep)],
                dst_ref=dst.at[:, where],
                send_sem=ss.at[o],
                recv_sem=rs.at[o],
                device_id=to,
                device_id_type=MESH,
            )
            for src, dst, where, ss, rs in (
                (can, out_ref, spot, send2, recv2),
                (canx, oux_ref, spotx, sendx, recvx),
            )
        ]

    copies = {}
    order = sorted(range(1, n_col), key=lambda o: abs(2 * o - n_col))
    for o in order:
        to = peer(row, col, 0, o)
        copies[o] = send_rows(to, step * to[1], mine, minex, o)
        for c in copies[o]:
            c.start()
    loads[3].wait()
    forms(lower_forms, lo, vo, vo_hbm, vsem)
    for c in stores:
        c.wait()
    for c in own:
        c.wait()
    for o in range(1, n_col):
        src = peer(row, col, 0, -o)
        spot = pl.ds(pl.multiple_of(cols * src[1], cols), cols)
        spotx = pl.ds(pl.multiple_of(8 * src[1], 8), 8)
        for c in copies[o]:
            c.wait_send()
        for c in send_rows(src, 0, spot, spotx, o):
            c.wait_recv()


def front(reach, latent, w1, b1, w2, b2, upper, lower):
    ch = w1.shape[2]
    rows, cols = latent.shape[0], latent.shape[1] // ch
    d = upper.shape[2]
    m = MARGIN
    high, wide, span = rows + 2 * m, cols + 2 * SIDE, cols + 2 * m
    n_col = lax.axis_size("col")
    tall = rows + 2
    deep = rows // n_col + 2
    left = 3 * (ch % 128)
    w1, w2 = (w.reshape(3, 3 * ch, ch) for w in (w1, w2))

    def around(full, thin):
        return [pltpu.VMEM((full // 2 if dr == 0 else thin, cols if dc == 0 else SIDE, ch), BF) for dr, dc in AROUND]

    return pl.pallas_call(
        front_kernel,
        out_shape=[
            jax.ShapeDtypeStruct((deep, n_col * cols, 256), BF),
            jax.ShapeDtypeStruct((deep, n_col * 8, 128), BF),
            jax.ShapeDtypeStruct((9, d, d), BF),
            jax.ShapeDtypeStruct((16, d, d), BF),
        ],
        in_specs=[SM, VM, HB, VM, HB, VM, HB, HB],
        out_specs=[HB, HB, HB, HB],
        scratch_shapes=around(rows, m)
        + around(tall, m + 1)
        + [
            pltpu.VMEM((rows, cols, ch), BF),
            pltpu.VMEM((2, rows // 2, SIDE, ch), BF),
            pltpu.VMEM((2, tall // 2, SIDE, ch), BF),
            pltpu.VMEM((pl.cdiv(ch, 128), rows * cols, 128), F32),
            pltpu.VMEM((high + 2, wide, ch), F32),
            pltpu.VMEM((high + 2, wide, ch), F32),
            pltpu.VMEM(((high + 2) * span, 3 * ch), BF),
            pltpu.VMEM(((high + 2) * span, left), F32),
            pltpu.VMEM((3, 3 * ch, ch), BF),
            pltpu.VMEM((3, 3 * ch, ch), BF),
            pltpu.VMEM((3 * ch, left), BF),
            pltpu.VMEM((3 * ch, left), BF),
            pltpu.VMEM((high, wide, ch), BF),
            pltpu.VMEM((tall, cols, 256), BF),
            pltpu.VMEM((tall, 8, 128), BF),
            pltpu.VMEM((tall, cols, 128), F32),
            pltpu.VMEM((3, 3, d, d), BF),
            pltpu.VMEM((3, 3, d, d), BF),
            pltpu.VMEM((9, d, d), BF),
            pltpu.VMEM((16, d, d), BF),
        ]
        + [pltpu.SemaphoreType.DMA((8,))] * 4
        + [
            pltpu.SemaphoreType.DMA((n_col,)),
            pltpu.SemaphoreType.DMA((n_col,)),
            pltpu.SemaphoreType.DMA((n_col,)),
            pltpu.SemaphoreType.DMA((n_col,)),
            pltpu.SemaphoreType.DMA((2,)),
            pltpu.SemaphoreType.DMA((4,)),
            pltpu.SemaphoreType.DMA((d // 64,)),
            pltpu.SemaphoreType.DMA((d // 64,)),
        ],
        compiler_params=pltpu.CompilerParams(
            collective_id=0, has_side_effects=True, vmem_limit_bytes=60 * 2**20
        ),
        name="front",
    )(reach, latent, w1, b1, w2, b2, upper, lower)


def decode_kernel(cols, d, can_hbm, canx_hbm, proj_ref, uup_hbm, bup_ref, ulo_hbm, blo_ref, out_ref,
                  hid, act, ts, acc, inter, projx, obuf, can_ref, canx_ref, uup, ulo, upsem, losem, osem, csem, xsem):
    row, col = lax.axis_index("row"), lax.axis_index("col")
    first_dev = (row == 0) & (col == 0)
    last_dev = (row == lax.axis_size("row") - 1) & (col == lax.axis_size("col") - 1)
    upc = [pltpu.make_async_copy(uup_hbm.at[i], uup.at[i], upsem.at[i]) for i in range(9)]
    loc = [pltpu.make_async_copy(ulo_hbm.at[i], ulo.at[i], losem.at[i]) for i in range(16)]
    rows_in = [
        (
            pltpu.make_async_copy(can_hbm.at[i], can_ref.at[i], csem.at[i]),
            pltpu.make_async_copy(canx_hbm.at[i], canx_ref.at[i], xsem.at[i]),
        )
        for i in range(4)
    ]
    for pair in rows_in:
        for c in pair:
            c.start()
    for i in (3, 4, 5, 6, 7, 8, 0, 1, 2):
        upc[i].start()
    for c in loc:
        c.start()
    body = pl.ds(PAD, cols)
    prev = pl.ds(PAD - 1, cols)
    nxt = pl.ds(PAD + 1, cols)
    zero8 = jnp.zeros((4, PAD, d), F32)
    hid[:, 0:PAD, :] = zero8
    hid[:, PAD + cols:, :] = zero8
    zact = jnp.zeros((6, 2, PAD, d), F32)
    act[:, :, 0:PAD, :] = zact
    act[:, :, PAD + cols:, :] = zact
    rest = proj_ref[256:]
    blank = jnp.zeros((64, d), BF)
    projx[0:64, 0:d] = rest
    projx[0:64, d : 2 * d] = blank
    projx[64:128, 0:d] = blank
    projx[64:128, d : 2 * d] = rest
    for i in range(4):
        for c in rows_in[i]:
            c.wait()
        extra = dot(canx_ref[i], projx[...])
        extra = jnp.concatenate(
            [extra[:, :d].reshape(cols // 16, 8, d), extra[:, d:].reshape(cols // 16, 8, d)], axis=1
        ).reshape(cols, d)
        v = (dot(can_ref[i], proj_ref[0:256]) + extra).astype(BF).astype(F32)
        hid[i, body, :] = v

    def three(load):
        mid = load(body)
        return [(load(prev) - mid).astype(BF), mid.astype(BF), (load(nxt) - mid).astype(BF)]

    def both(x, p):
        s = dot(x[1], uup[3 * p + 1])
        return s + dot(x[0], uup[3 * p]), s + dot(x[2], uup[3 * p + 2])

    def middle(k):
        e, o = both(three(lambda sl: hid[k, sl, :]), 1)
        ts[k % 2, 0] = e + bup_ref[...]
        ts[k % 2, 1] = o + bup_ref[...]

    def act_row(slot, par, v):
        half = 0.5 * v
        act[slot, par, body, :] = half + half * jnp.tanh(half)

    for i in (3, 4, 5):
        upc[i].wait()
    middle(0)
    for i in (6, 7, 8, 0, 1, 2):
        upc[i].wait()

    def step(k, _):
        x = three(lambda sl: hid[k + 1, sl, :] - hid[k, sl, :])
        down = both(x, 2)
        for par in range(2):
            act_row(2 * k, par, ts[k % 2, par] + down[par])
        middle(k + 1)
        up = both(x, 0)
        for par in range(2):
            act_row(2 * k + 1, par, ts[(k + 1) % 2, par] - up[par])
        return 0

    lax.fori_loop(0, 3, step, 0)

    @pl.when(first_dev)
    def _():
        act[0, :, body, :] = jnp.zeros((2, cols, d), F32)

    @pl.when(last_dev)
    def _():
        act[5, :, body, :] = jnp.zeros((2, cols, d), F32)

    for c in loc:
        c.wait()

    def products(r):
        one, two, sgn = ((0, 2, -1), (1, 2, 1), (2, 1, -1), (1, 3, -1))[r]
        vs = [[], [], [], []]
        for t in range(2):

            def ld(par, sl):
                u, v = act[2 * t + one, par, sl, :], act[2 * t + two, par, sl, :]
                return u + v if sgn > 0 else u - v

            ev = ld(0, body)
            od = ld(1, body)
            vs[0].append((ld(1, prev) - od).astype(BF))
            vs[1].append((ev + od).astype(BF))
            vs[2].append((od - ev).astype(BF))
            vs[3].append((ev - ld(0, nxt)).astype(BF))
        m = [dot(jnp.concatenate(vs[c], axis=0), ulo[4 * r + c]) for c in range(4)]
        plus, minus = m[1] + m[2], m[1] - m[2]
        y = [plus + m[0], minus - m[3]]
        return [[y[b][t * cols : (t + 1) * cols] for b in range(2)] for t in range(2)]

    ocp = [pltpu.make_async_copy(obuf.at[i], out_ref.at[i], osem.at[i]) for i in range(4)]

    def emit(t, a, b, v):
        for lane in range(0, d, 128):
            inter[2 * t + a, lane // 128, pl.ds(b, cols, stride=2), :] = v[:, lane : lane + 128]

    def flush(a):
        for t in range(2):
            for lane in range(0, d, 128):
                obuf[2 * t + a, :, lane : lane + 128] = inter[2 * t + a, lane // 128].astype(BF)
            ocp[2 * t + a].start()

    def inner_pair(_, carry):
        y = products(1)
        for t in range(2):
            h = hid[t + 1, body, :] + blo_ref[...]
            for b in range(2):
                v = h + y[t][b]
                acc[t, 0, b] = v
                acc[t, 1, b] = v
        y = products(2)
        for t in range(2):
            for b in range(2):
                acc[t, 0, b] += y[t][b]
                acc[t, 1, b] -= y[t][b]
        return carry

    def outer_pair(_, carry):
        y = products(0)
        for t in range(2):
            for b in range(2):
                emit(t, 0, b, acc[t, 0, b] + y[t][b])
        flush(0)
        y = products(3)
        for t in range(2):
            for b in range(2):
                emit(t, 1, b, acc[t, 1, b] - y[t][b])
        flush(1)
        return carry

    once = 1 + row // lax.axis_size("row")
    lax.fori_loop(0, once, inner_pair, 0)
    outer_pair(0, 0)
    for c in ocp:
        c.wait()


def decode(canvas, extra, proj, uup, bup, ulo, blo):
    cols, d = canvas.shape[1], proj.shape[1]
    return pl.pallas_call(
        functools.partial(decode_kernel, cols, d),
        out_shape=jax.ShapeDtypeStruct((4, 2 * cols, d), BF),
        in_specs=[HB, HB, VM, HB, VM, HB, VM],
        out_specs=HB,
        scratch_shapes=[
            pltpu.VMEM((4, cols + 2 * PAD, d), F32),
            pltpu.VMEM((6, 2, cols + 2 * PAD, d), F32),
            pltpu.VMEM((2, 2, cols, d), F32),
            pltpu.VMEM((2, 2, 2, cols, d), F32),
            pltpu.VMEM((4, d // 128, 2 * cols, 128), F32),
            pltpu.VMEM((128, 2 * d), BF),
            pltpu.VMEM((4, 2 * cols, d), BF),
            pltpu.VMEM(canvas.shape, BF),
            pltpu.VMEM(extra.shape, BF),
            pltpu.VMEM((9, d, d), BF),
            pltpu.VMEM((16, d, d), BF),
            pltpu.SemaphoreType.DMA((9,)),
            pltpu.SemaphoreType.DMA((16,)),
            pltpu.SemaphoreType.DMA((4,)),
            pltpu.SemaphoreType.DMA((4,)),
            pltpu.SemaphoreType.DMA((4,)),
        ],
        compiler_params=pltpu.CompilerParams(vmem_limit_bytes=60 * 2**20),
        name="decode",
    )(canvas, extra, proj, uup, bup, ulo, blo)


def on_device(
    latent,
    tile_reach,
    first_weight,
    first_bias,
    second_weight,
    second_bias,
    proj_weight,
    upper_weight,
    upper_bias,
    lower_weight,
    lower_bias,
):
    canvas, extra, uup, ulo = front(
        tile_reach.transpose(0, 2, 1),
        latent,
        first_weight,
        first_bias,
        second_weight,
        second_bias,
        upper_weight,
        lower_weight,
    )
    return decode(canvas, extra, proj_weight, uup, upper_bias[None], ulo, lower_bias[None])


def solution(mesh):
    in_specs = (P("row", "col"), P(), P(), P(), P(), P(), P(), P(), P(), P(), P())
    out_specs = P(("row", "col"), None, None)
    return jax.shard_map(on_device, mesh=mesh, in_specs=in_specs, out_specs=out_specs, check_vma=False)
```

```python
import functools

import jax
import jax.numpy as jnp
from jax import lax
from jax.experimental import pallas as pl
from jax.experimental.pallas import tpu as pltpu
from jax.sharding import PartitionSpec as P

MARGIN = 4
SIDE = 8
PAD = 8
F32 = jnp.float32
BF = jnp.bfloat16
MESH = pl.DeviceIdType.MESH
VM = pl.BlockSpec(memory_space=pltpu.VMEM)
HB = pl.BlockSpec(memory_space=pltpu.HBM)
SM = pl.BlockSpec(memory_space=pltpu.SMEM)
AROUND = [(dr, dc) for dr in (-1, 0, 1) for dc in (-1, 0, 1) if (dr, dc) != (0, 0)]


def dot(a, b):
    return jnp.dot(a, b, preferred_element_type=F32)


def peer(row, col, dr, dc):
    rows, cols = lax.axis_size("row"), lax.axis_size("col")
    return lax.rem(row + (dr + rows), rows), lax.rem(col + (dc + cols), cols)


def place(reach_ref, row, col, dr, dc, rows, cols):
    n_row, n_col = lax.axis_size("row"), lax.axis_size("col")
    there = (row + dr >= 0) & (row + dr < n_row) & (col + dc >= 0) & (col + dc < n_col)
    r = lax.rem(row + (dr + n_row), n_row)
    c = lax.rem(col + (dc + n_col), n_col)
    low_r = jnp.maximum((row + dr) * rows - reach_ref[r, 0, c], 0)
    high_r = jnp.minimum((row + dr + 1) * rows + reach_ref[r, 1, c], rows * n_row)
    low_c = jnp.maximum((col + dc) * cols - reach_ref[r, 2, c], 0)
    high_c = jnp.minimum((col + dc + 1) * cols + reach_ref[r, 3, c], cols * n_col)
    return low_r, jnp.where(there, high_r, low_r), low_c, high_c


def spread(g):
    outer = 0.5 * (g[0] + g[2])
    mid = 0.5 * g[1]
    return [g[0], outer + mid, outer - mid, g[2]]


def upper_forms(up, out, sl, ln):
    cols = []
    for b in range(3):
        w = [up[a, b, sl, ln].astype(F32) for a in range(3)]
        cols.append([w[0], w[0] + w[1] + w[2], w[2]])
    for p in range(3):
        v = [cols[0][p], cols[0][p] + cols[1][p] + cols[2][p], cols[2][p]]
        for q in range(3):
            out[3 * p + q, sl, ln] = v[q].astype(BF)


def lower_forms(lo, out, sl, ln):
    cols = [spread([lo[a, b, sl, ln].astype(F32) for a in range(3)]) for b in range(3)]
    for r in range(4):
        v = spread([cols[b][r] for b in range(3)])
        for c in range(4):
            out[4 * r + c, sl, ln] = v[c].astype(BF)


def front_kernel(
    reach_ref, lat_ref, w1_hbm, b1_ref, w2_hbm, b2_ref, up_hbm, lo_hbm, out_ref, oux_ref, uo_hbm, vo_hbm, *refs
):
    lands, strips = refs[:8], refs[8:16]
    core_ref, side, side2, stage, x, act, ga, rest, w1, w2, r1, r2, y_ref, can, canx, count_ref, up, lo, uo, vo = refs[16:36]
    send0, recv0, send, recv, send2, recv2, sendx, recvx, self_sem, wsem, usem, vsem = refs[36:]
    rows, cols, ch = core_ref.shape
    m = MARGIN
    high, wide, span = rows + 2 * m, cols + 2 * SIDE, cols + 2 * m
    base = SIDE - m
    main = ch // 128 * 128
    left = ch - main
    part = 8
    row, col = lax.axis_index("row"), lax.axis_index("col")
    n_col = lax.axis_size("col")
    barrier = pltpu.get_barrier_semaphore()
    greet = [peer(row, col, 0, o) for o in range(1, n_col)]
    greet += [peer(row, col, dr, dc) for dr, dc in AROUND if dr != 0]
    for g in greet:
        pl.semaphore_signal(barrier, inc=1, device_id=g, device_id_type=MESH)
    loads = [
        pltpu.make_async_copy(src, dst, wsem.at[n])
        for n, (src, dst) in enumerate(((w1_hbm, w1), (w2_hbm, w2), (up_hbm, up), (lo_hbm, lo)))
    ]
    for c in loads[:2]:
        c.start()
    low_r, high_r, low_c, high_c = place(reach_ref, row, col, 0, 0, rows, cols)
    top, start = row * rows - m, col * cols - SIDE

    def put(dr, dc, at, num, value):
        lo_c, hi_c = {-1: (0, SIDE), 0: (SIDE, SIDE + cols), 1: (SIDE + cols, wide)}[dc]
        rid = lax.broadcasted_iota(jnp.int32, value.shape, 0) + (top + at)
        cid = lax.broadcasted_iota(jnp.int32, value.shape, 1) + (start + lo_c)
        ok = (rid >= low_r) & (rid < high_r) & (cid >= low_c) & (cid < high_c)
        x[pl.ds(at + 1, num), lo_c:hi_c] = jnp.where(ok, value.astype(F32), 0.0)

    def put_core(n, _):
        put(0, 0, m + part * n, part, core_ref[pl.ds(part * n, part)])
        return 0

    for c in range(cols):
        v = lat_ref[:, ch * c : ch * (c + 1)].astype(F32)
        for n in range(pl.cdiv(ch, 128)):
            size = min(128, ch - 128 * n)
            piece = v[:, 128 * n : 128 * n + size]
            if size < 128:
                piece = jnp.concatenate([piece, jnp.zeros((rows, 128 - size), F32)], axis=1)
            stage[n, pl.ds(c, rows, stride=cols), :] = piece
    for n in range(pl.cdiv(ch, 128)):
        size = min(128, ch - 128 * n)
        core_ref[:, :, 128 * n : 128 * n + size] = stage[n].reshape(rows, cols, 128)[:, :, :size].astype(BF)

    def turned(v):
        return jnp.concatenate([v[:, 4:8], v[:, 0:4]], axis=1)

    mid_row = rows // 2
    for n, at in ((0, cols - SIDE), (1, 0)):
        v = core_ref[:, at : at + SIDE].astype(F32)
        lo_half, hi_half = (turned(v[:mid_row]), v[mid_row:]) if n == 0 else (v[:mid_row], turned(v[mid_row:]))
        low_lanes = lax.broadcasted_iota(jnp.int32, lo_half.shape, 1) < m
        side[n] = jnp.where(low_lanes, lo_half, hi_half).astype(BF)
    pl.semaphore_wait(barrier, len(greet))
    halos = []
    for n, (dr, dc) in enumerate(AROUND):
        rs = {-1: pl.ds(rows - m, m), 0: pl.ds(0, rows), 1: pl.ds(0, m)}[dr]
        cs = {-1: pl.ds(cols - SIDE, SIDE), 0: pl.ds(0, cols), 1: pl.ds(0, SIDE)}[dc]
        halos.append(
            pltpu.make_async_remote_copy(
                src_ref=core_ref.at[rs, cs] if dr != 0 else side.at[0 if dc < 0 else 1],
                dst_ref=lands[n],
                send_sem=send0.at[n],
                recv_sem=recv0.at[n],
                device_id=peer(row, col, -dr, -dc),
                device_id_type=MESH,
            )
        )
        halos[-1].start()
    for c in loads[2:]:
        c.start()
    lax.fori_loop(0, rows // part, put_core, 0)
    for buf in (x, act):
        buf[0] = jnp.zeros((wide, ch), F32)
        buf[high + 1] = jnp.zeros((wide, ch), F32)

    def clear(n, _):
        act[pl.ds(part * n + 1, part), 0:8, :] = jnp.zeros((part, 8, ch), F32)
        act[pl.ds(part * n + 1, part), wide - 8 : wide, :] = jnp.zeros((part, 8, ch), F32)
        return 0

    lax.fori_loop(0, high // part, clear, 0)
    shape = count_ref.shape
    rid = lax.broadcasted_iota(jnp.int32, shape, 0) + (row * rows - 1)
    cid = lax.broadcasted_iota(jnp.int32, shape, 1) + col * cols
    total = jnp.zeros(shape, F32)
    for dr in (-1, 0, 1):
        for dc in (-1, 0, 1):
            lr, hr, lc, hc = place(reach_ref, row, col, dr, dc, rows, cols)
            inside = (rid >= lr) & (rid < hr) & (cid >= lc) & (cid < hc)
            total += jnp.where(inside, 1.0, 0.0)
    count_ref[...] = total

    def narrow(w, r):
        r[...] = jnp.concatenate([w[dr, :, main:] for dr in range(3)], axis=1)

    for c in loads[:2]:
        c.wait()
    narrow(w1, r1)
    narrow(w2, r2)
    for c in halos:
        c.wait()
    got = dict(zip(AROUND, lands))
    for dr, dc in AROUND:
        if dr == 0:

            def put_side(n, _):
                v = got[0, dc][pl.ds(part * n, part)].astype(F32)
                pair = (turned(v), v) if dc < 0 else (v, turned(v))
                put(0, dc, m + part * n, part, pair[0])
                put(0, dc, m + mid_row + part * n, part, pair[1])
                return 0

            lax.fori_loop(0, mid_row // part, put_side, 0)
        else:
            put(dr, dc, 0 if dr < 0 else m + rows, m, got[dr, dc][...])

    def gather(buf):
        def group(n, _):
            for k in range(3):
                at = 6 * n + 2 * k
                pieces = [
                    buf[pl.ds(at, 2), base + dc : base + dc + span, :].reshape(2 * span, ch) for dc in (-1, 0, 1)
                ]
                v = jnp.concatenate(pieces, axis=1).astype(BF)
                ga[pl.ds(pl.multiple_of(span * at, 16), 2 * span), :] = v
            return 0

        lax.fori_loop(0, (high + 2) // 6, group, 0)

    half = high // 2
    count = half * span

    def conv(w, r, b_ref, finish):
        for n in range(2):
            size = (high + 2) // 2 * span
            rest[pl.ds(n * size, size), :] = dot(ga[pl.ds(n * size, size), :], r[...])

        for n in range(2):
            at = n * count
            big = (
                dot(ga[pl.ds(at, count), :], w[0, :, :main])
                + dot(ga[pl.ds(at + span, count), :], w[1, :, :main])
                + dot(ga[pl.ds(at + 2 * span, count), :], w[2, :, :main])
            )
            finish(n, 0, main, big + b_ref[:main][None])
            small = (
                rest[pl.ds(at, count), :left]
                + rest[pl.ds(at + span, count), left : 2 * left]
                + rest[pl.ds(at + 2 * span, count), 2 * left :]
            )
            finish(n, main, ch, small + b_ref[main:][None])

    def window_mask(n, width):
        rid = lax.broadcasted_iota(jnp.int32, (half, 1, width), 0) + (top + n * half)
        kid = lax.broadcasted_iota(jnp.int32, (1, span, width), 1) + (start + base)
        row_one = jnp.where((rid >= low_r) & (rid < high_r), 1.0, 0.0)
        col_one = jnp.where((kid >= low_c) & (kid < high_c), 1.0, 0.0)
        return row_one * col_one

    def first(n, lo, hi, v):
        v = 0.5 * v
        v = (v + v * jnp.tanh(v)).reshape(half, span, hi - lo)
        act[pl.ds(n * half + 1, half), base : base + span, lo:hi] = v * window_mask(n, hi - lo)

    def second(n, lo, hi, v):
        here = pl.ds(n * half + 1, half)
        v = v.reshape(half, span, hi - lo) + x[here, base : base + span, lo:hi]
        act[here, base : base + span, lo:hi] = v * window_mask(n, hi - lo)

    gather(x)
    conv(w1, r1, b1_ref, first)
    gather(act)
    conv(w2, r2, b2_ref, second)

    def emit(n, _):
        y_ref[pl.ds(part * n, part)] = act[pl.ds(part * n + 1, part)].astype(BF)
        return 0

    lax.fori_loop(0, high // part, emit, 0)
    edge = m + 1
    tall = rows + 2
    cut = tall // 2
    for n, at in ((0, SIDE + cols), (1, 0)):
        v = act[pl.ds(m, cut), at : at + SIDE] + turned(act[pl.ds(m + cut, cut), at : at + SIDE])
        side2[n] = v.astype(BF)
    copies = []
    for n, (dr, dc) in enumerate(AROUND):
        rs = {-1: pl.ds(high - edge, edge), 0: pl.ds(m - 1, tall), 1: pl.ds(0, edge)}[dr]
        cs = {-1: pl.ds(SIDE + cols, SIDE), 0: pl.ds(SIDE, cols), 1: pl.ds(0, SIDE)}[dc]
        copies.append(
            pltpu.make_async_remote_copy(
                src_ref=y_ref.at[rs, cs] if dr != 0 else side2.at[0 if dc < 0 else 1],
                dst_ref=strips[n],
                send_sem=send.at[n],
                recv_sem=recv.at[n],
                device_id=peer(row, col, -dr, -dc),
                device_id_type=MESH,
            )
        )
        copies[-1].start()
    depth, width = up.shape[2:]
    block = 64
    stores = []

    def forms(form, src, dst, dst_hbm, sem):
        def store(n):
            sl = pl.ds(pl.multiple_of(n * block, block), block)
            return pltpu.make_async_copy(dst.at[:, sl], dst_hbm.at[:, sl], sem.at[n])

        def body(n, _):
            def inner(k, _):
                sl = pl.ds(pl.multiple_of(n * block + k * 16, 16), 16)
                for lane in range(0, width, 128):
                    form(src, dst, sl, slice(lane, lane + 128))
                return 0

            lax.fori_loop(0, block // 16, inner, 0)
            store(n).start()
            return 0

        lax.fori_loop(0, depth // block, body, 0)
        stores.extend(store(n) for n in range(depth // block))

    loads[2].wait()
    forms(upper_forms, up, uo, uo_hbm, usem)
    for c in copies:
        c.wait()
    got2 = dict(zip(AROUND, strips))

    main = 256

    def merge(lo_r, num, dr):
        here = pl.ds(lo_r, num)
        total = y_ref[pl.ds(m - 1 + lo_r, num), SIDE : SIDE + cols].astype(F32)
        late = lo_r >= cut
        there = pl.ds(lo_r - cut if late else lo_r, num)
        lhs, rhs = got2[0, -1][there].astype(F32), got2[0, 1][there].astype(F32)
        if late:
            lhs, rhs = turned(lhs), turned(rhs)
        low = lax.broadcasted_iota(jnp.int32, lhs.shape, 1) < m
        lhs, rhs = jnp.where(low, lhs, 0.0), jnp.where(low, 0.0, rhs)
        if dr:
            total += got2[dr, 0][...].astype(F32)
            lhs += got2[dr, -1][...].astype(F32)
            rhs += got2[dr, 1][...].astype(F32)
        total += jnp.concatenate([lhs, rhs], axis=1)
        n = count_ref[here][:, :, :1]
        total = jnp.where(n > 0, total / jnp.maximum(n, 1.0), 0.0)
        can[here] = total[:, :, :main].astype(BF)
        canx[here] = jnp.concatenate([total[:, :8, main:], total[:, 8:, main:]], axis=2).astype(BF)

    merge(0, edge, -1)
    merge(edge, cut - edge, 0)
    merge(cut, cut - edge, 0)
    merge(tall - edge, edge, 1)
    mine = pl.ds(pl.multiple_of(cols * col, cols), cols)
    step = rows // n_col
    deep = step + 2
    minex = pl.ds(pl.multiple_of(8 * col, 8), 8)
    own = [
        pltpu.make_async_copy(can.at[pl.ds(step * col, deep)], out_ref.at[:, mine], self_sem.at[0]),
        pltpu.make_async_copy(canx.at[pl.ds(step * col, deep)], oux_ref.at[:, minex], self_sem.at[1]),
    ]
    for c in own:
        c.start()

    def send_rows(to, at, spot, spotx, o):
        return [
            pltpu.make_async_remote_copy(
                src_ref=src.at[pl.ds(at, deep)],
                dst_ref=dst.at[:, where],
                send_sem=ss.at[o],
                recv_sem=rs.at[o],
                device_id=to,
                device_id_type=MESH,
            )
            for src, dst, where, ss, rs in (
                (can, out_ref, spot, send2, recv2),
                (canx, oux_ref, spotx, sendx, recvx),
            )
        ]

    copies = {}
    order = sorted(range(1, n_col), key=lambda o: abs(2 * o - n_col))
    for o in order:
        to = peer(row, col, 0, o)
        copies[o] = send_rows(to, step * to[1], mine, minex, o)
        for c in copies[o]:
            c.start()
    loads[3].wait()
    forms(lower_forms, lo, vo, vo_hbm, vsem)
    for c in stores:
        c.wait()
    for c in own:
        c.wait()
    for o in range(1, n_col):
        src = peer(row, col, 0, -o)
        spot = pl.ds(pl.multiple_of(cols * src[1], cols), cols)
        spotx = pl.ds(pl.multiple_of(8 * src[1], 8), 8)
        for c in copies[o]:
            c.wait_send()
        for c in send_rows(src, 0, spot, spotx, o):
            c.wait_recv()


def front(reach, latent, w1, b1, w2, b2, upper, lower):
    ch = w1.shape[2]
    rows, cols = latent.shape[0], latent.shape[1] // ch
    d = upper.shape[2]
    m = MARGIN
    high, wide, span = rows + 2 * m, cols + 2 * SIDE, cols + 2 * m
    n_col = lax.axis_size("col")
    tall = rows + 2
    deep = rows // n_col + 2
    left = 3 * (ch % 128)
    w1, w2 = (w.reshape(3, 3 * ch, ch) for w in (w1, w2))

    def around(full, thin):
        return [pltpu.VMEM((full // 2 if dr == 0 else thin, cols if dc == 0 else SIDE, ch), BF) for dr, dc in AROUND]

    return pl.pallas_call(
        front_kernel,
        out_shape=[
            jax.ShapeDtypeStruct((deep, n_col * cols, 256), BF),
            jax.ShapeDtypeStruct((deep, n_col * 8, 128), BF),
            jax.ShapeDtypeStruct((9, d, d), BF),
            jax.ShapeDtypeStruct((16, d, d), BF),
        ],
        in_specs=[SM, VM, HB, VM, HB, VM, HB, HB],
        out_specs=[HB, HB, HB, HB],
        scratch_shapes=around(rows, m)
        + around(tall, m + 1)
        + [
            pltpu.VMEM((rows, cols, ch), BF),
            pltpu.VMEM((2, rows // 2, SIDE, ch), BF),
            pltpu.VMEM((2, tall // 2, SIDE, ch), BF),
            pltpu.VMEM((pl.cdiv(ch, 128), rows * cols, 128), F32),
            pltpu.VMEM((high + 2, wide, ch), F32),
            pltpu.VMEM((high + 2, wide, ch), F32),
            pltpu.VMEM(((high + 2) * span, 3 * ch), BF),
            pltpu.VMEM(((high + 2) * span, left), F32),
            pltpu.VMEM((3, 3 * ch, ch), BF),
            pltpu.VMEM((3, 3 * ch, ch), BF),
            pltpu.VMEM((3 * ch, left), BF),
            pltpu.VMEM((3 * ch, left), BF),
            pltpu.VMEM((high, wide, ch), BF),
            pltpu.VMEM((tall, cols, 256), BF),
            pltpu.VMEM((tall, 8, 128), BF),
            pltpu.VMEM((tall, cols, 128), F32),
            pltpu.VMEM((3, 3, d, d), BF),
            pltpu.VMEM((3, 3, d, d), BF),
            pltpu.VMEM((9, d, d), BF),
            pltpu.VMEM((16, d, d), BF),
        ]
        + [pltpu.SemaphoreType.DMA((8,))] * 4
        + [
            pltpu.SemaphoreType.DMA((n_col,)),
            pltpu.SemaphoreType.DMA((n_col,)),
            pltpu.SemaphoreType.DMA((n_col,)),
            pltpu.SemaphoreType.DMA((n_col,)),
            pltpu.SemaphoreType.DMA((2,)),
            pltpu.SemaphoreType.DMA((4,)),
            pltpu.SemaphoreType.DMA((d // 64,)),
            pltpu.SemaphoreType.DMA((d // 64,)),
        ],
        compiler_params=pltpu.CompilerParams(
            collective_id=0, has_side_effects=True, vmem_limit_bytes=60 * 2**20
        ),
        name="front",
    )(reach, latent, w1, b1, w2, b2, upper, lower)


def decode_kernel(cols, d, can_ref, canx_ref, proj_ref, uup_hbm, bup_ref, ulo_hbm, blo_ref, out_ref,
                  hid, act, ts, acc, inter, projx, obuf, uup, ulo, upsem, losem, osem):
    row, col = lax.axis_index("row"), lax.axis_index("col")
    first_dev = (row == 0) & (col == 0)
    last_dev = (row == lax.axis_size("row") - 1) & (col == lax.axis_size("col") - 1)
    upc = [pltpu.make_async_copy(uup_hbm.at[i], uup.at[i], upsem.at[i]) for i in range(9)]
    loc = [pltpu.make_async_copy(ulo_hbm.at[i], ulo.at[i], losem.at[i]) for i in range(16)]
    for i in (3, 4, 5, 6, 7, 8, 0, 1, 2):
        upc[i].start()
    for c in loc:
        c.start()
    body = pl.ds(PAD, cols)
    prev = pl.ds(PAD - 1, cols)
    nxt = pl.ds(PAD + 1, cols)
    zero8 = jnp.zeros((4, PAD, d), F32)
    hid[:, 0:PAD, :] = zero8
    hid[:, PAD + cols:, :] = zero8
    zact = jnp.zeros((6, 2, PAD, d), F32)
    act[:, :, 0:PAD, :] = zact
    act[:, :, PAD + cols:, :] = zact
    rest = proj_ref[256:]
    blank = jnp.zeros((64, d), BF)
    projx[0:64, 0:d] = rest
    projx[0:64, d : 2 * d] = blank
    projx[64:128, 0:d] = blank
    projx[64:128, d : 2 * d] = rest
    for i in range(4):
        extra = dot(canx_ref[i], projx[...])
        extra = jnp.concatenate(
            [extra[:, :d].reshape(cols // 16, 8, d), extra[:, d:].reshape(cols // 16, 8, d)], axis=1
        ).reshape(cols, d)
        v = (dot(can_ref[i], proj_ref[0:256]) + extra).astype(BF).astype(F32)
        hid[i, body, :] = v

    def three(load):
        mid = load(body)
        return [(load(prev) - mid).astype(BF), mid.astype(BF), (load(nxt) - mid).astype(BF)]

    def both(x, p):
        s = dot(x[1], uup[3 * p + 1])
        return s + dot(x[0], uup[3 * p]), s + dot(x[2], uup[3 * p + 2])

    def middle(k):
        e, o = both(three(lambda sl: hid[k, sl, :]), 1)
        ts[k % 2, 0] = e + bup_ref[...]
        ts[k % 2, 1] = o + bup_ref[...]

    def act_row(slot, par, v):
        half = 0.5 * v
        act[slot, par, body, :] = half + half * jnp.tanh(half)

    for i in (3, 4, 5):
        upc[i].wait()
    middle(0)
    for i in (6, 7, 8, 0, 1, 2):
        upc[i].wait()

    def step(k, _):
        x = three(lambda sl: hid[k + 1, sl, :] - hid[k, sl, :])
        down = both(x, 2)
        for par in range(2):
            act_row(2 * k, par, ts[k % 2, par] + down[par])
        middle(k + 1)
        up = both(x, 0)
        for par in range(2):
            act_row(2 * k + 1, par, ts[(k + 1) % 2, par] - up[par])
        return 0

    lax.fori_loop(0, 3, step, 0)

    @pl.when(first_dev)
    def _():
        act[0, :, body, :] = jnp.zeros((2, cols, d), F32)

    @pl.when(last_dev)
    def _():
        act[5, :, body, :] = jnp.zeros((2, cols, d), F32)

    for c in loc:
        c.wait()

    def products(r):
        one, two, sgn = ((0, 2, -1), (1, 2, 1), (2, 1, -1), (1, 3, -1))[r]
        vs = [[], [], [], []]
        for t in range(2):

            def ld(par, sl):
                u, v = act[2 * t + one, par, sl, :], act[2 * t + two, par, sl, :]
                return u + v if sgn > 0 else u - v

            ev = ld(0, body)
            od = ld(1, body)
            vs[0].append((ld(1, prev) - od).astype(BF))
            vs[1].append((ev + od).astype(BF))
            vs[2].append((od - ev).astype(BF))
            vs[3].append((ev - ld(0, nxt)).astype(BF))
        m = [dot(jnp.concatenate(vs[c], axis=0), ulo[4 * r + c]) for c in range(4)]
        plus, minus = m[1] + m[2], m[1] - m[2]
        y = [plus + m[0], minus - m[3]]
        return [[y[b][t * cols : (t + 1) * cols] for b in range(2)] for t in range(2)]

    ocp = [pltpu.make_async_copy(obuf.at[i], out_ref.at[i], osem.at[i]) for i in range(4)]

    def emit(t, a, b, v):
        for lane in range(0, d, 128):
            inter[2 * t + a, lane // 128, pl.ds(b, cols, stride=2), :] = v[:, lane : lane + 128]

    def flush(a):
        for t in range(2):
            for lane in range(0, d, 128):
                obuf[2 * t + a, :, lane : lane + 128] = inter[2 * t + a, lane // 128].astype(BF)
            ocp[2 * t + a].start()

    def inner_pair(_, carry):
        y = products(1)
        for t in range(2):
            h = hid[t + 1, body, :] + blo_ref[...]
            for b in range(2):
                v = h + y[t][b]
                acc[t, 0, b] = v
                acc[t, 1, b] = v
        y = products(2)
        for t in range(2):
            for b in range(2):
                acc[t, 0, b] += y[t][b]
                acc[t, 1, b] -= y[t][b]
        return carry

    def outer_pair(_, carry):
        y = products(0)
        for t in range(2):
            for b in range(2):
                emit(t, 0, b, acc[t, 0, b] + y[t][b])
        flush(0)
        y = products(3)
        for t in range(2):
            for b in range(2):
                emit(t, 1, b, acc[t, 1, b] - y[t][b])
        flush(1)
        return carry

    once = 1 + row // lax.axis_size("row")
    lax.fori_loop(0, once, inner_pair, 0)
    outer_pair(0, 0)
    for c in ocp:
        c.wait()


def decode(canvas, extra, proj, uup, bup, ulo, blo):
    cols, d = canvas.shape[1], proj.shape[1]
    return pl.pallas_call(
        functools.partial(decode_kernel, cols, d),
        out_shape=jax.ShapeDtypeStruct((4, 2 * cols, d), BF),
        in_specs=[VM, VM, VM, HB, VM, HB, VM],
        out_specs=HB,
        scratch_shapes=[
            pltpu.VMEM((4, cols + 2 * PAD, d), F32),
            pltpu.VMEM((6, 2, cols + 2 * PAD, d), F32),
            pltpu.VMEM((2, 2, cols, d), F32),
            pltpu.VMEM((2, 2, 2, cols, d), F32),
            pltpu.VMEM((4, d // 128, 2 * cols, 128), F32),
            pltpu.VMEM((128, 2 * d), BF),
            pltpu.VMEM((4, 2 * cols, d), BF),
            pltpu.VMEM((9, d, d), BF),
            pltpu.VMEM((16, d, d), BF),
            pltpu.SemaphoreType.DMA((9,)),
            pltpu.SemaphoreType.DMA((16,)),
            pltpu.SemaphoreType.DMA((4,)),
        ],
        compiler_params=pltpu.CompilerParams(vmem_limit_bytes=60 * 2**20),
        name="decode",
    )(canvas, extra, proj, uup, bup, ulo, blo)


def on_device(
    latent,
    tile_reach,
    first_weight,
    first_bias,
    second_weight,
    second_bias,
    proj_weight,
    upper_weight,
    upper_bias,
    lower_weight,
    lower_bias,
):
    canvas, extra, uup, ulo = front(
        tile_reach.transpose(0, 2, 1),
        latent,
        first_weight,
        first_bias,
        second_weight,
        second_bias,
        upper_weight,
        lower_weight,
    )
    return decode(canvas, extra, proj_weight, uup, upper_bias[None], ulo, lower_bias[None])


def solution(mesh):
    in_specs = (P("row", "col"), P(), P(), P(), P(), P(), P(), P(), P(), P(), P())
    out_specs = P(("row", "col"), None, None)
    return jax.shard_map(on_device, mesh=mesh, in_specs=in_specs, out_specs=out_specs, check_vma=False)
```
